256 devices in a mesh: seq: 64 (over z, x, core), tp: 4 (over y).
Axes of the slice: x: 4, y: 4, z: 8, core: 2. Of those that a mesh axis runs over, the one named last changes fastest.
Arguments:
- prompt_keys: bfloat16 [64, 16384, 512], P(None, 'seq', 'tp'), may hold values from -6 to 16
- prompt_values: bfloat16 [64, 16384, 512], P(None, 'seq', 'tp'), may hold values from -6 to 6
- keep_mask: int32 [64, 128, 4], P(None, 'seq', 'tp'), may hold values from 0 to 1, as said below
- owner_sequence: int32 [64], replicated, may hold values from 0 to 63, each once
- step_queries: bfloat16 [64, 16, 4, 1024], P('seq', None, 'tp'), may hold values from -15 to 26
- new_keys: bfloat16 [64, 16, 512], P('seq', None, 'tp'), may hold values from -12 to 12
- new_values: bfloat16 [64, 16, 512], P('seq', None, 'tp'), may hold values from -6 to 6
Outputs:
- attended: bfloat16 [64, 16, 4, 1024], P('seq', None, 'tp')
The draws below stay inside these ranges and needn't reach their ends.
Inputs may be any that keep to these rules, and one draw needn't show every extreme that they name: `keep_mask`: the last block of every sequence is kept for every head; every sequence and head keeps between 32 and 96 blocks.
All inputs are finite; a program needn't handle non-finite values.
Results may differ from the reference program's by a relative error of at most 0.009.
The reference program's roundings to bfloat16 on the way count: a program that leaves them out, or rounds other values in their place, can miss the bound.
Values may be sent and summed in bfloat16 or wider, within the bound.
A program may use at most 128 MiB of HBM per device.

```python
import math
import jax
import jax.numpy as jnp
from jax import lax

DH = 128
KVH = 4
QG = 8
BLOCK = 128
STEPS = 16
LEN = 16384
SEQS = 64
NB = 128
KEEP = 96


def draw_keep_mask(key, part):
    count_key, score_key = jax.random.split(jax.random.fold_in(key, 11))
    counts = jax.random.randint(count_key, (SEQS, KVH), NB // 4, KEEP + 1)
    counts = counts.at[0, 0].set(KEEP).at[SEQS - 1, KVH - 1].set(NB // 4)
    block_index = jnp.arange(NB).astype(jnp.int32)
    scores = jax.random.randint(score_key, (SEQS, NB, KVH), 0, 4 * NB) + 2 * block_index[None, :, None]
    scores = jnp.where(block_index[None, :, None] == NB - 1, 10 * NB, scores)
    scores = scores * NB + block_index[None, :, None]
    ordering = jnp.argsort(-scores, axis=1, stable=True)
    ranking = jnp.argsort(ordering, axis=1, stable=True)
    return (ranking < counts[:, None, :]).astype(jnp.int32)


def draw_prompt_keys(key, part):
    shape_all = (SEQS, LEN, KVH * DH)
    normal_part = jnp.clip(jax.random.normal(jax.random.fold_in(key, 21), shape_all, jnp.float32), -6.0, 6.0)
    return normal_part.astype(jnp.bfloat16)


def draw_step_queries(key, part):
    shape_all = (SEQS, STEPS, KVH, QG * DH)
    normal_part = jnp.clip(2.5 * jax.random.normal(jax.random.fold_in(key, 31), shape_all, jnp.float32), -15.0, 15.0)
    return normal_part.astype(jnp.bfloat16)


def levels(stream_key, dims, shards, smallest, top_value):
    def one(dim, parts):
        draws = jax.random.uniform(jax.random.fold_in(jax.random.fold_in(stream_key, 6), dim), (parts,), jnp.float32, smallest / len(shards), top_value / len(shards))
        return jnp.repeat(jnp.exp(draws), dims[dim] // parts).reshape((-1,) + (1,) * (len(dims) - dim - 1))

    factor_of = one(*shards[0])
    for cut in shards[1:]:
        factor_of = factor_of * one(*cut)
    return factor_of


def noise(stream_key, extent, deviation, most, cuts=(), held_as=jnp.bfloat16):
    values = deviation * jax.random.normal(stream_key, extent, jnp.float32)
    if cuts:
        values = values * levels(stream_key, extent, cuts, -0.22, 0.18)
    return jnp.clip(values, -most, most).astype(held_as)


def setup_inputs(seed: int = 0) -> dict:
    key_list = jax.random.split(jax.random.key(seed), 8)
    prompt_keys = draw_prompt_keys(jax.random.fold_in(key_list[7], 71), 0)
    prompt_values = noise(key_list[1], (SEQS, LEN, KVH * DH), 1.0, 6.0, ((1, 64), (2, 4)))
    keep_mask = draw_keep_mask(jax.random.fold_in(key_list[7], 71), 0)
    owner_sequence = jax.random.permutation(key_list[3], SEQS).astype(jnp.int32)
    step_queries = draw_step_queries(jax.random.fold_in(key_list[7], 71), 0)
    new_keys = noise(key_list[5], (SEQS, STEPS, KVH * DH), 2.0, 12.0, ((0, 64), (2, 4)))
    new_values = noise(key_list[6], (SEQS, STEPS, KVH * DH), 1.0, 6.0, ((0, 64), (2, 4)))
    return dict(prompt_keys=prompt_keys, prompt_values=prompt_values, keep_mask=keep_mask, owner_sequence=owner_sequence, step_queries=step_queries, new_keys=new_keys, new_values=new_values)


floor_score = -1e+30

def frequencies(half_width):
    position_index = jnp.arange(half_width).astype(jnp.float32)
    base_rate = jnp.exp(position_index * (-2.0 / (2 * half_width)) * math.log(500000.0))
    wavelength = 2.0 * math.pi / base_rate
    smooth = (8192.0 / wavelength - 1.0) / 3.0
    blended = (1.0 - smooth) * base_rate / 8.0 + smooth * base_rate
    return jnp.where(wavelength < 2048.0, base_rate, jnp.where(wavelength > 8192.0, base_rate / 8.0, blended))

def rotate(vector, offset):
    half_width = vector.shape[-1] // 2
    angles = offset.astype(jnp.float32)[..., None] * frequencies(half_width)
    cosine = jnp.cos(angles)
    sine_part = jnp.sin(angles)
    lower_half = vector[..., :half_width]
    upper_half = vector[..., half_width:]
    return jnp.concatenate([lower_half * cosine - upper_half * sine_part, upper_half * cosine + lower_half * sine_part], axis=-1)

def select_blocks(mask_column):
    running = jnp.cumsum(mask_column).astype(jnp.int32)
    slot_index = jnp.arange(KEEP).astype(jnp.int32)
    chosen = lax.optimization_barrier(jnp.sum((running[None, :] <= slot_index[:, None]).astype(jnp.int32), axis=1)).astype(jnp.int32)
    chosen = jnp.minimum(chosen, mask_column.shape[0] - 1).astype(jnp.int32)
    live_slots = slot_index < running[-1]
    return (chosen, live_slots, ((slot_index - chosen) * BLOCK).astype(jnp.int32))

def attend(query_rows, cached_keys, cached_values, live_tokens, fresh_keys, fresh_values, groups):
    score_scale = 1.0 / math.sqrt(query_rows.shape[-1])
    older = jnp.dot(query_rows, cached_keys.T, preferred_element_type=jnp.float32) * score_scale
    older = jnp.where(live_tokens[None, :], older, floor_score)
    new_scores = jnp.dot(query_rows, fresh_keys.T, preferred_element_type=jnp.float32) * score_scale
    row_step = jnp.arange(query_rows.shape[0]) // groups
    causal = row_step[:, None] >= jnp.arange(fresh_keys.shape[0])[None, :]
    new_scores = jnp.where(causal, new_scores, floor_score)
    highest = jnp.maximum(lax.optimization_barrier(jnp.max(older, axis=1)), lax.optimization_barrier(jnp.max(new_scores, axis=1)))
    older_weight = jnp.where(live_tokens[None, :], jnp.exp(older - highest[:, None]), 0.0)
    newer_weight = jnp.where(causal, jnp.exp(new_scores - highest[:, None]), 0.0)
    row_total = lax.optimization_barrier(jnp.sum(older_weight, axis=1)) + lax.optimization_barrier(jnp.sum(newer_weight, axis=1))
    result = jnp.dot((older_weight / row_total[:, None]).astype(jnp.bfloat16), cached_values, preferred_element_type=jnp.float32)
    result = result + jnp.dot((newer_weight / row_total[:, None]).astype(jnp.bfloat16), fresh_values, preferred_element_type=jnp.float32)
    return result

def reference(prompt_keys, prompt_values, keep_mask, owner_sequence, step_queries, new_keys, new_values):

    def one_owner(owner_rank):
        sequence = owner_sequence[owner_rank]
        mask_rows = keep_mask[sequence]
        counts = lax.optimization_barrier(jnp.sum(mask_rows, axis=0)).astype(jnp.int32)
        first_position = (jnp.max(counts) * BLOCK).astype(jnp.int32)
        positions = first_position + jnp.arange(STEPS).astype(jnp.int32)
        key_blocks = prompt_keys[sequence].reshape(NB, BLOCK, KVH, DH)
        value_blocks = prompt_values[sequence].reshape(NB, BLOCK, KVH, DH)
        query_all = step_queries[owner_rank].reshape(STEPS, KVH, QG, DH)
        fresh_all = new_keys[owner_rank].reshape(STEPS, KVH, DH)
        fresh_vals = new_values[owner_rank].reshape(STEPS, KVH, DH)
        outputs = []
        for head_index in range(KVH):
            chosen, live_slots, offset = select_blocks(mask_rows[:, head_index])
            picked = jnp.take(key_blocks[:, :, head_index], chosen, axis=0)
            turned = rotate(picked.astype(jnp.float32), offset[:, None]).astype(jnp.bfloat16).reshape(KEEP * BLOCK, DH)
            kept_values = jnp.take(value_blocks[:, :, head_index], chosen, axis=0).reshape(KEEP * BLOCK, DH)
            live_tokens = jnp.repeat(live_slots, BLOCK)
            query_rows = rotate(query_all[:, head_index].astype(jnp.float32), positions[:, None]).astype(jnp.bfloat16).reshape(STEPS * QG, DH)
            fresh_turned = rotate(fresh_all[:, head_index].astype(jnp.float32), positions).astype(jnp.bfloat16)
            result = attend(query_rows, turned, kept_values, live_tokens, fresh_turned, fresh_vals[:, head_index], QG)
            outputs.append(result.reshape(STEPS, QG * DH))
        return jnp.stack(outputs, axis=1).astype(jnp.bfloat16)
    return lax.map(one_owner, jnp.arange(SEQS).astype(jnp.int32))
```

```python
import functools
import math

import jax
import jax.numpy as jnp
from jax import lax
from jax.experimental import pallas as pl
from jax.experimental.pallas import tpu as pltpu
from jax.sharding import PartitionSpec as P

BLOCK = 128
HEAD = 128
NEG = -1e30
MESH = pl.DeviceIdType.MESH
F32 = jnp.float32
BF16 = jnp.bfloat16


def frequencies(half_width):
    position_index = jnp.arange(half_width).astype(jnp.float32)
    base_rate = jnp.exp(position_index * (-2.0 / (2 * half_width)) * math.log(500000.0))
    wavelength = 2.0 * math.pi / base_rate
    smooth = (8192.0 / wavelength - 1.0) / 3.0
    blended = (1.0 - smooth) * base_rate / 8.0 + smooth * base_rate
    return jnp.where(
        wavelength < 2048.0, base_rate, jnp.where(wavelength > 8192.0, base_rate / 8.0, blended)
    )


def kernel(
    nz, nx, ny,
    owner_ref, flags_ref, freq_ref, query_ref, newk_ref, newv_ref, keys_hbm, values_hbm,
    out_ref,
    keys, values, queries, counts, totals, table, live, pair_out, pair_in, pair_own,
    x_out, x_in, x_own, z_out, z_in, z_own,
    load_sem, c1_send, c1_recv, c2_send, c2_recv, t_send, t_recv,
    qz_send, qz_recv, qx_send, qx_recv, qc_send, qc_recv,
    pair_send, pair_recv, x_send, x_recv, z_send, z_recv,
):
    seqs = nz * nx * 2
    group = nx * 2
    tokens = 2 * BLOCK
    steps = newk_ref.shape[0]
    heads = query_ref.shape[1] // HEAD
    rows = steps * heads
    score_scale = math.log2(math.e) / math.sqrt(HEAD)

    me = lax.axis_index("seq")
    tp = lax.axis_index("tp")
    z = me // group
    x = (me // 2) % nx
    c = me % 2
    sib = 1 - c

    def dev(z_, x_, c_):
        return (z_ * nx + x_) * 2 + c_

    def far(i):
        half = nz // 2
        return (half + (i % 2) * (nz - (i + 1) // 2) + (1 - i % 2) * (i // 2)) % nz

    def remote(src, dst, send, recv, where, where_tp=None):
        return pltpu.make_async_remote_copy(
            src_ref=src, dst_ref=dst, send_sem=send, recv_sem=recv,
            device_id=(where, tp if where_tp is None else where_tp), device_id_type=MESH,
        )

    chunk = seqs // nz

    def load(i, which):
        src, dst = ((keys_hbm, keys), (values_hbm, values))[which]
        part = pl.ds(i * chunk, chunk)
        return pltpu.make_async_copy(src.at[part], dst.at[part], load_sem.at[which, i])

    for i in range(nz):
        load(i, 0).start()
        load(i, 1).start()

    counts[me] = flags_ref[0:1, :] + flags_ref[1:2, :]
    for g in range(heads):
        queries[me, g * steps:(g + 1) * steps, :] = query_ref[:, g * HEAD:(g + 1) * HEAD]

    barrier = pltpu.get_barrier_semaphore()
    near = z * group
    xc = x * 2 + c
    for r in range(1, group):
        pl.semaphore_signal(barrier, inc=1, device_id=(near + (xc + r) % group, tp), device_id_type=MESH)
    for d in range(1, nz):
        pl.semaphore_signal(barrier, inc=1, device_id=(dev((z + d) % nz, x, c), tp), device_id_type=MESH)
    for d in range(1, ny):
        pl.semaphore_signal(barrier, inc=1, device_id=(me, (tp + d) % ny), device_id_type=MESH)
    pl.semaphore_wait(barrier, group - 1 + nz - 1 + ny - 1)

    def counts_near(r):
        return remote(counts.at[me], counts.at[me], c1_send.at[r], c1_recv.at[r], near + (xc + r) % group)

    def counts_near_in(r):
        slot = near + (xc - r + group) % group
        return remote(counts.at[slot], counts.at[slot], c1_send.at[r], c1_recv.at[r], slot)

    def counts_far(d):
        part = pl.ds(z * group, group)
        return remote(counts.at[part], counts.at[part], c2_send.at[d], c2_recv.at[d], dev((z + d) % nz, x, c))

    def counts_far_in(d):
        z_ = (z - d + nz) % nz
        part = pl.ds(z_ * group, group)
        return remote(counts.at[part], counts.at[part], c2_send.at[d], c2_recv.at[d], dev(z_, x, c))

    def query_z(i):
        return remote(queries.at[me], queries.at[me], qz_send.at[i], qz_recv.at[i],
                      dev((z - far(i) + nz) % nz, x, c))

    def query_z_in(i):
        slot = dev((z + far(i)) % nz, x, c)
        return remote(queries.at[slot], queries.at[slot], qz_send.at[i], qz_recv.at[i], slot)

    def query_x(i, d):
        slot = dev((z + far(i)) % nz, x, c)
        return remote(queries.at[slot], queries.at[slot], qx_send.at[i, d], qx_recv.at[i, d],
                      dev(z, (x + d) % nx, c))

    def query_x_in(i, d):
        x_ = (x - d + nx) % nx
        slot = dev((z + far(i)) % nz, x_, c)
        return remote(queries.at[slot], queries.at[slot], qx_send.at[i, d], qx_recv.at[i, d], dev(z, x_, c))

    def query_c(i, d):
        slot = dev((z + far(i)) % nz, (x - d + nx) % nx, c)
        return remote(queries.at[slot], queries.at[slot], qc_send.at[i, d], qc_recv.at[i, d], dev(z, x, sib))

    def query_c_in(i, d):
        slot = dev((z + far(i)) % nz, (x - d + nx) % nx, sib)
        return remote(queries.at[slot], queries.at[slot], qc_send.at[i, d], qc_recv.at[i, d], dev(z, x, sib))

    def forward_z(i):
        for d in range(1, nx):
            query_x(i, d).start()
        query_c(i, 0).start()

    def forward_x(i):
        for d in range(1, nx):
            query_x_in(i, d).wait_recv()
            query_c(i, d).start()

    for r in range(1, group):
        counts_near(r).start()
    for i in range(nz - 1):
        query_z(i).start()
    for r in range(1, group):
        counts_near_in(r).wait_recv()
    for d in range(1, nz):
        counts_far(d).start()
    forward_z(nz - 1)
    for d in range(1, nz):
        counts_far_in(d).wait_recv()

    before = jnp.zeros((1, HEAD), F32)
    total = jnp.zeros((1, HEAD), F32)
    for j in range(seqs):
        row = counts[j]
        total = total + row
        before = before + jnp.where(j < me, row, 0.0)
    totals[tp] = total
    for d in range(1, ny):
        remote(totals.at[tp], totals.at[tp], t_send.at[d], t_recv.at[d], me, (tp + d) % ny).start()

    freq = freq_ref[...]
    lane = lax.broadcasted_iota(jnp.int32, (1, HEAD), 1)
    sign = jnp.where(lane < HEAD // 2, -1.0, 1.0).astype(F32)

    def down(row):
        return jnp.transpose(jnp.broadcast_to(row, (HEAD, HEAD)))[:seqs]

    slot0 = before
    slot1 = before + flags_ref[0:1, :]
    first_block = (2 * me).astype(F32)
    for j, slot in enumerate((slot0, slot1)):
        angle = (down(slot) - (first_block + j)) * float(BLOCK) * freq
        table[2 * j] = jnp.cos(angle)
        table[2 * j + 1] = jnp.sin(angle) * sign
        live[j] = down(flags_ref[j:j + 1, :])

    def rotate_keys(i, carry):
        for j in range(2):
            cosine = table[2 * j, pl.ds(i, 1), :]
            sine = table[2 * j + 1, pl.ds(i, 1), :]
            part = pl.ds(j * BLOCK, BLOCK)
            stored = keys[i, part, :].astype(F32)
            turned = stored * cosine + pltpu.roll(stored, HEAD // 2, 1) * sine
            keys[i, part, :] = turned.astype(BF16)
        return carry

    for i in range(nz):
        load(i, 0).wait()
        lax.fori_loop(i * chunk, (i + 1) * chunk, rotate_keys, 0)
        if i < nz - 1:
            query_z_in(i).wait_recv()
            forward_z(i)
    for i in range(nz):
        load(i, 1).wait()

    longest = total
    for d in range(1, ny):
        slot = (tp - d + ny) % ny
        remote(totals.at[slot], totals.at[slot], t_send.at[d], t_recv.at[d], me, slot).wait_recv()
    for d in range(1, ny):
        longest = jnp.maximum(longest, totals[(tp + d) % ny])
    angle = down(longest) * float(BLOCK) * freq
    table[4] = jnp.cos(angle)
    table[5] = jnp.sin(angle)
    step_angle = lax.broadcasted_iota(jnp.int32, (steps, HEAD), 0).astype(F32) * freq
    step_cos = jnp.cos(step_angle)
    step_sin = jnp.sin(step_angle)

    def step_turn(s):
        cosine = table[4, pl.ds(s, 1), :]
        sine = table[5, pl.ds(s, 1), :]
        return (
            cosine * step_cos - sine * step_sin,
            (sine * step_cos + cosine * step_sin) * sign,
        )

    def turn_queries(slot, s):
        cosine, sine = step_turn(s)
        stored = queries[slot].astype(F32)
        swapped = pltpu.roll(stored, HEAD // 2, 1)
        shape = (heads, steps, HEAD)
        turned = stored.reshape(shape) * cosine[None] + swapped.reshape(shape) * sine[None]
        return turned.reshape(rows, HEAD).astype(BF16)

    def contract(a, b, dims):
        return lax.dot_general(a, b, (dims, ((), ())), preferred_element_type=F32)

    def shifted(m):
        return m.astype(BF16).astype(F32)

    def partial(slot):
        s = owner_ref[slot]
        turned = turn_queries(slot, s)
        scores = contract(keys[s], turned, ((1,), (1,))) * score_scale
        tops, pieces = [], []
        for j in range(2):
            pieces.append(scores[j * BLOCK:(j + 1) * BLOCK])
            kept = live[j, pl.ds(s, 1), :] > 0.5
            tops.append((kept, jnp.where(kept, jnp.max(pieces[j], axis=0, keepdims=True), NEG)))
        m = shifted(jnp.maximum(tops[0][1], tops[1][1]))
        weights = [
            jnp.exp2(pieces[j] - jnp.where(tops[j][0], m, -NEG)) for j in range(2)
        ]
        l = jnp.sum(weights[0] + weights[1], axis=0, keepdims=True)
        weights = jnp.concatenate(weights, axis=0).astype(BF16)
        return m, l, contract(values[s], weights, ((0,), (0,)))

    sub8 = lax.broadcasted_iota(jnp.int32, (8, HEAD), 0)
    sub16 = lax.broadcasted_iota(jnp.int32, (16, HEAD), 0)

    def put(ref, m, l, o):
        ref[0:HEAD, :] = o
        ref[HEAD:HEAD + 8, :] = jnp.where(sub8 == 0, m, l)

    def get(ref):
        return ref[HEAD:HEAD + 1, :], ref[HEAD + 1:HEAD + 2, :], ref[0:HEAD, :]

    def put_half(ref, m, l, o):
        high = l.astype(BF16).astype(F32)
        ref[0:HEAD, :] = o.astype(BF16)
        tail = jnp.where(sub16 == 0, m, jnp.where(sub16 == 1, high, l - high))
        ref[HEAD:HEAD + 16, :] = tail.astype(BF16)

    def get_half(ref):
        tail = ref[HEAD:HEAD + 16, :].astype(F32)
        return tail[0:1], tail[1:2] + tail[2:3], ref[0:HEAD, :].astype(F32)

    def merge(parts):
        m = functools.reduce(jnp.maximum, [p[0] for p in parts])
        scales = [jnp.exp2(p[0] - m) for p in parts]
        l = functools.reduce(jnp.add, [p[1] * a for p, a in zip(parts, scales)])
        o = functools.reduce(jnp.add, [p[2] * a for p, a in zip(parts, scales)])
        return m, l, o

    def pair_copy(i):
        return remote(pair_out.at[i], pair_in.at[i], pair_send.at[i], pair_recv.at[i], dev(z, x, sib))

    def x_copy(i, d):
        return remote(x_out.at[i, d], x_in.at[i, d], x_send.at[i, d], x_recv.at[i, d],
                      dev(z, (x + d) % nx, c))

    def z_copy(i):
        return remote(z_out.at[i], z_in.at[i], z_send.at[i], z_recv.at[i], dev((z + far(i)) % nz, x, c))

    def stage_partials(i):
        z_ = (z + far(i)) % nz
        for d in range(nx):
            query_c_in(i, d).wait_recv()
        for d in range(nx):
            put(pair_out.at[i, d], *partial(dev(z_, (x + d) % nx, sib)))
        pair_copy(i).start()
        for d in range(nx):
            put(pair_own.at[i, d], *partial(dev(z_, (x + d) % nx, c)))

    def stage_x(i):
        pair_copy(i).wait_recv()
        for d in range(nx):
            merged = merge([get(pair_own.at[i, d]), get(pair_in.at[i, d])])
            if d == 0:
                put(x_own.at[i], *merged)
            else:
                put_half(x_out.at[i, d], *merged)
                x_copy(i, d).start()

    def stage_z(i):
        for d in range(1, nx):
            x_copy(i, d).wait_recv()
        merged = merge([get(x_own.at[i])] + [get_half(x_in.at[i, d]) for d in range(1, nx)])

        @pl.when(i < nz - 1)
        def _():
            put_half(z_out.at[i], *merged)
            z_copy(i).start()

        @pl.when(i == nz - 1)
        def _():
            put(z_own, *merged)

    forward_x(0)

    def step(i, carry):
        @pl.when(i < nz - 1)
        def _():
            forward_x(i + 1)

        @pl.when(i < nz)
        def _():
            stage_partials(i)

        @pl.when((i >= 1) & (i < nz + 1))
        def _():
            stage_x(i - 1)

        @pl.when(i >= 2)
        def _():
            stage_z(i - 2)

        return carry

    lax.fori_loop(0, nz + 2, step, 0)

    s = owner_ref[me]
    turned = turn_queries(me, s)
    cosine, sine = step_turn(s)
    fresh = newk_ref[...].astype(F32)
    fresh = (fresh * cosine + pltpu.roll(fresh, HEAD // 2, 1) * sine).astype(BF16)
    scores = contract(fresh, turned, ((1,), (1,))) * score_scale
    row_step = lax.broadcasted_iota(jnp.int32, (steps, rows), 1) % steps
    causal = lax.broadcasted_iota(jnp.int32, (steps, rows), 0) <= row_step
    scores = jnp.where(causal, scores, NEG)
    m = shifted(jnp.max(scores, axis=0, keepdims=True))
    weights = jnp.where(causal, jnp.exp2(scores - m), 0.0)
    l = jnp.sum(weights, axis=0, keepdims=True)
    parts = [(m, l, contract(newv_ref[...], weights.astype(BF16), ((0,), (0,))))]

    for i in range(nz - 1):
        z_copy(i).wait_recv()
        parts.append(get_half(z_in.at[i]))
    parts.append(get(z_own))
    m, l, o = merge(parts)
    result = jnp.transpose(o / l).astype(BF16)
    for g in range(heads):
        out_ref[:, g * HEAD:(g + 1) * HEAD] = result[g * steps:(g + 1) * steps]

    for r in range(1, group):
        counts_near(r).wait_send()
    for d in range(1, nz):
        counts_far(d).wait_send()
    for d in range(1, ny):
        remote(totals.at[tp], totals.at[tp], t_send.at[d], t_recv.at[d], me, (tp + d) % ny).wait_send()
    for i in range(nz):
        if i < nz - 1:
            query_z(i).wait_send()
            z_copy(i).wait_send()
        pair_copy(i).wait_send()
        for d in range(nx):
            query_c(i, d).wait_send()
            if d:
                query_x(i, d).wait_send()
                x_copy(i, d).wait_send()


def shards(
    nz, nx, ny,
    prompt_keys, prompt_values, keep_mask, owner_sequence, step_queries, new_keys, new_values,
):
    seqs = prompt_keys.shape[0]
    steps = step_queries.shape[1]
    flags = jnp.pad(keep_mask[:, :, 0].astype(F32).T, ((0, 0), (0, HEAD - seqs)))
    freq = frequencies(HEAD // 2)
    freq = jnp.concatenate([freq, freq])[None]
    any_spec = pl.BlockSpec(memory_space=pl.ANY)
    vmem = pl.BlockSpec(memory_space=pltpu.VMEM)
    dma = pltpu.SemaphoreType.DMA
    group = nx * 2
    out = pl.pallas_call(
        functools.partial(kernel, nz, nx, ny),
        out_shape=jax.ShapeDtypeStruct((steps, step_queries.shape[3]), BF16),
        in_specs=[pl.BlockSpec(memory_space=pltpu.SMEM)] + [vmem] * 5 + [any_spec] * 2,
        out_specs=vmem,
        scratch_shapes=[
            pltpu.VMEM((seqs, 2 * BLOCK, HEAD), BF16),
            pltpu.VMEM((seqs, 2 * BLOCK, HEAD), BF16),
            pltpu.VMEM((seqs, HEAD, HEAD), BF16),
            pltpu.VMEM((seqs, 1, HEAD), F32),
            pltpu.VMEM((ny, 1, HEAD), F32),
            pltpu.VMEM((6, seqs, HEAD), F32),
            pltpu.VMEM((2, seqs, HEAD), F32),
            pltpu.VMEM((nz, nx, HEAD + 8, HEAD), F32),
            pltpu.VMEM((nz, nx, HEAD + 8, HEAD), F32),
            pltpu.VMEM((nz, nx, HEAD + 8, HEAD), F32),
            pltpu.VMEM((nz, nx, HEAD + 16, HEAD), BF16),
            pltpu.VMEM((nz, nx, HEAD + 16, HEAD), BF16),
            pltpu.VMEM((nz, HEAD + 8, HEAD), F32),
            pltpu.VMEM((nz, HEAD + 16, HEAD), BF16),
            pltpu.VMEM((nz, HEAD + 16, HEAD), BF16),
            pltpu.VMEM((HEAD + 8, HEAD), F32),
            dma((2, nz)),
            dma((group,)), dma((group,)), dma((nz,)), dma((nz,)), dma((ny,)), dma((ny,)),
            dma((nz,)), dma((nz,)), dma((nz, nx)), dma((nz, nx)), dma((nz, nx)), dma((nz, nx)),
            dma((nz,)), dma((nz,)), dma((nz, nx)), dma((nz, nx)), dma((nz,)), dma((nz,)),
        ],
        compiler_params=pltpu.CompilerParams(
            collective_id=0, has_side_effects=True, vmem_limit_bytes=48 * 1024 * 1024
        ),
    )(
        owner_sequence, flags, freq, step_queries[0, :, 0], new_keys[0], new_values[0],
        prompt_keys, prompt_values,
    )
    return out[None, :, None]


def solution(mesh):
    in_specs = (
        P(None, "seq", "tp"),
        P(None, "seq", "tp"),
        P(None, "seq", "tp"),
        P(),
        P("seq", None, "tp", None),
        P("seq", None, "tp"),
        P("seq", None, "tp"),
    )
    out_specs = P("seq", None, "tp", None)
    seq = mesh.shape["seq"]
    nx = 4 if seq >= 64 else 2
    body = functools.partial(shards, seq // (2 * nx), nx, mesh.shape["tp"])
    return jax.shard_map(body, mesh=mesh, in_specs=in_specs, out_specs=out_specs, check_vma=False)
```

```python
import functools
import math

import jax
import jax.numpy as jnp
from jax import lax
from jax.experimental import pallas as pl
from jax.experimental.pallas import tpu as pltpu
from jax.sharding import PartitionSpec as P

BLOCK = 128
HEAD = 128
NEG = -1e30
LAG = 4
MESH = pl.DeviceIdType.MESH
F32 = jnp.float32
BF16 = jnp.bfloat16


def frequencies(half_width):
    position_index = jnp.arange(half_width).astype(jnp.float32)
    base_rate = jnp.exp(position_index * (-2.0 / (2 * half_width)) * math.log(500000.0))
    wavelength = 2.0 * math.pi / base_rate
    smooth = (8192.0 / wavelength - 1.0) / 3.0
    blended = (1.0 - smooth) * base_rate / 8.0 + smooth * base_rate
    return jnp.where(
        wavelength < 2048.0, base_rate, jnp.where(wavelength > 8192.0, base_rate / 8.0, blended)
    )


def kernel(
    nz, nx, ny,
    owner_hbm, mask_hbm, freq_ref, query_hbm, newk_hbm, newv_hbm, keys_hbm, values_hbm,
    out_ref,
    owner_ref, mask_ref, query_ref, newk_ref, newv_ref,
    keys, values, queries, counts, totals, table, live, pair_out, pair_in, pair_own,
    x_out, x_in, x_own, z_out, z_in, z_own,
    load_sem, small_sem, send_sem, c1_recv, c2_recv, t_recv,
    qz_recv, qx_recv, qc_recv, pair_recv, x_recv, z_recv,
):
    seqs = nz * nx * 2
    group = nx * 2
    tokens = 2 * BLOCK
    steps = newk_ref.shape[0]
    heads = query_ref.shape[1] // HEAD
    rows = steps * heads
    score_scale = math.log2(math.e) / math.sqrt(HEAD)

    me = lax.axis_index("seq")
    tp = lax.axis_index("tp")
    z = me // group
    x = (me // 2) % nx
    c = me % 2
    sib = 1 - c

    def dev(z_, x_, c_):
        return (z_ * nx + x_) * 2 + c_

    def far(i):
        half = nz // 2
        return (half + (i % 2) * (nz - (i + 1) // 2) + (1 - i % 2) * (i // 2)) % nz

    def remote(ref, dst, send, recv, where, where_tp=None):
        return pltpu.make_async_remote_copy(
            src_ref=ref, dst_ref=dst, send_sem=send_sem.at[send], recv_sem=recv,
            device_id=(where, tp if where_tp is None else where_tp), device_id_type=MESH,
        )

    def drain(ref, sem):
        pltpu.make_async_copy(ref, ref, sem).wait()

    chunks = 4 if seqs > 8 else 2
    chunk = seqs // chunks

    def load(i):
        part = pl.ds(i * chunk, chunk)
        return pltpu.make_async_copy(keys_hbm.at[part], keys.at[part], load_sem.at[i])

    load_values = pltpu.make_async_copy(values_hbm, values, load_sem.at[chunks])
    small = [
        pltpu.make_async_copy(src, dst, small_sem.at[i])
        for i, (src, dst) in enumerate((
            (mask_hbm, mask_ref), (query_hbm, query_ref), (owner_hbm, owner_ref),
            (newk_hbm, newk_ref), (newv_hbm, newv_ref),
        ))
    ]
    for copy in small:
        copy.start()
    for i in range(chunks):
        load(i).start()
    load_values.start()

    small[0].wait()
    flags = [mask_ref[j].astype(F32) for j in range(2)]
    counts[me] = flags[0] + flags[1]
    small[1].wait()
    for g in range(heads):
        queries[me, g * steps:(g + 1) * steps, :] = query_ref[:, g * HEAD:(g + 1) * HEAD]

    barrier = pltpu.get_barrier_semaphore()
    near = z * group
    xc = x * 2 + c
    for r in range(1, group):
        pl.semaphore_signal(barrier, inc=1, device_id=(near + (xc + r) % group, tp), device_id_type=MESH)
    for d in range(1, nz):
        pl.semaphore_signal(barrier, inc=1, device_id=(dev((z + d) % nz, x, c), tp), device_id_type=MESH)
    for d in range(1, ny):
        pl.semaphore_signal(barrier, inc=1, device_id=(me, (tp + d) % ny), device_id_type=MESH)
    pl.semaphore_wait(barrier, group - 1 + nz - 1 + ny - 1)

    def counts_near(r):
        return remote(counts.at[me], counts.at[me], 0, c1_recv, near + (xc + r) % group)

    def counts_far(d):
        part = pl.ds(near, group)
        return remote(counts.at[part], counts.at[part], 1, c2_recv, dev((z + d) % nz, x, c))

    def totals_out(d):
        return remote(totals.at[tp], totals.at[tp], 2, t_recv, me, (tp + d) % ny)

    def query(slot, recv, where):
        return remote(queries.at[slot], queries.at[slot], 3, recv, where)

    def query_z(i):
        return query(me, qz_recv.at[i], dev((z - far(i) + nz) % nz, x, c))

    def query_z_in(i):
        slot = dev((z + far(i)) % nz, x, c)
        return query(slot, qz_recv.at[i], slot)

    def query_x(i, d):
        return query(dev((z + far(i)) % nz, x, c), qx_recv.at[i], dev(z, (x + d) % nx, c))

    def query_c(i, d):
        slot = dev((z + far(i)) % nz, (x - d + nx) % nx, c)
        return query(slot, qc_recv.at[i], dev(z, x, sib))

    def forward_z(i):
        for d in range(1, nx):
            query_x(i, d).start()
        query_c(i, 0).start()

    def forward_x(i):
        drain(queries.at[pl.ds(0, nx - 1)], qx_recv.at[i])
        for d in range(1, nx):
            query_c(i, d).start()

    for r in range(1, group):
        counts_near(r).start()
    for i in range(nz - 1):
        query_z(i).start()
    forward_z(nz - 1)
    drain(counts.at[pl.ds(0, group - 1)], c1_recv)
    for d in range(1, nz):
        counts_far(d).start()
    for i in range(nz - 1):
        query_z_in(i).wait_recv()
        forward_z(i)
    drain(counts.at[pl.ds(0, (nz - 1) * group)], c2_recv)

    before = jnp.zeros((1, seqs), F32)
    total = jnp.zeros((1, seqs), F32)
    for j in range(seqs):
        row = counts[j]
        total = total + row
        before = before + jnp.where(j < me, row, 0.0)
    totals[tp] = total
    for d in range(1, ny):
        totals_out(d).start()

    freq = freq_ref[...]
    lane = lax.broadcasted_iota(jnp.int32, (1, HEAD), 1)
    sign = jnp.where(lane < HEAD // 2, -1.0, 1.0).astype(F32)

    def down(row):
        return jnp.transpose(jnp.broadcast_to(row, (HEAD, seqs)))

    slot0 = before
    slot1 = before + flags[0]
    first_block = (2 * me).astype(F32)
    for j, slot in enumerate((slot0, slot1)):
        angle = (down(slot) - (first_block + j)) * float(BLOCK) * freq
        table[2 * j] = jnp.cos(angle)
        table[2 * j + 1] = jnp.sin(angle) * sign
        live[j] = down(flags[j])

    def rotate_keys(i, carry):
        for j in range(2):
            cosine = table[2 * j, pl.ds(i, 1), :]
            sine = table[2 * j + 1, pl.ds(i, 1), :]
            part = pl.ds(j * BLOCK, BLOCK)
            stored = keys[i, part, :].astype(F32)
            turned = stored * cosine + pltpu.roll(stored, HEAD // 2, 1) * sine
            keys[i, part, :] = turned.astype(BF16)
        return carry

    for i in range(chunks):
        load(i).wait()
        lax.fori_loop(i * chunk, (i + 1) * chunk, rotate_keys, 0)
    load_values.wait()

    for copy in small[2:]:
        copy.wait()

    longest = total
    drain(totals.at[pl.ds(0, ny - 1)], t_recv)
    for d in range(1, ny):
        longest = jnp.maximum(longest, totals[(tp + d) % ny])
    angle = down(longest) * float(BLOCK) * freq
    table[4] = jnp.cos(angle)
    table[5] = jnp.sin(angle)
    step_angle = lax.broadcasted_iota(jnp.int32, (steps, HEAD), 0).astype(F32) * freq
    step_cos = jnp.cos(step_angle)
    step_sin = jnp.sin(step_angle)

    def step_turn(s):
        cosine = table[4, pl.ds(s, 1), :]
        sine = table[5, pl.ds(s, 1), :]
        return (
            cosine * step_cos - sine * step_sin,
            (sine * step_cos + cosine * step_sin) * sign,
        )

    def turn_queries(slot, s):
        cosine, sine = step_turn(s)
        stored = queries[slot].astype(F32)
        swapped = pltpu.roll(stored, HEAD // 2, 1)
        shape = (heads, steps, HEAD)
        turned = stored.reshape(shape) * cosine[None] + swapped.reshape(shape) * sine[None]
        return turned.reshape(rows, HEAD).astype(BF16)

    def contract(a, b, dims):
        return lax.dot_general(a, b, (dims, ((), ())), preferred_element_type=F32)

    def shifted(m):
        return m.astype(BF16).astype(F32)

    def partial(slot):
        s = owner_ref[slot]
        turned = turn_queries(slot, s)
        scores = contract(keys[s], turned, ((1,), (1,))) * score_scale
        tops, pieces = [], []
        for j in range(2):
            pieces.append(scores[j * BLOCK:(j + 1) * BLOCK])
            kept = live[j, pl.ds(s, 1), :] > 0.5
            tops.append((kept, jnp.where(kept, jnp.max(pieces[j], axis=0, keepdims=True), NEG)))
        m = shifted(jnp.maximum(tops[0][1], tops[1][1]))
        weights = [
            jnp.exp2(pieces[j] - jnp.where(tops[j][0], m, -NEG)) for j in range(2)
        ]
        l = jnp.sum(weights[0] + weights[1], axis=0, keepdims=True)
        weights = jnp.concatenate(weights, axis=0).astype(BF16)
        return m, l, contract(values[s], weights, ((0,), (0,)))

    sub8 = lax.broadcasted_iota(jnp.int32, (8, HEAD), 0)
    sub16 = lax.broadcasted_iota(jnp.int32, (16, HEAD), 0)

    def put(ref, m, l, o):
        ref[0:HEAD, :] = o
        ref[HEAD:HEAD + 8, :] = jnp.where(sub8 == 0, m, l)

    def get(ref):
        return ref[HEAD:HEAD + 1, :], ref[HEAD + 1:HEAD + 2, :], ref[0:HEAD, :]

    def put_half(ref, m, l, o):
        high = l.astype(BF16).astype(F32)
        ref[0:HEAD, :] = o.astype(BF16)
        tail = jnp.where(sub16 == 0, m, jnp.where(sub16 == 1, high, l - high))
        ref[HEAD:HEAD + 16, :] = tail.astype(BF16)

    def get_half(ref):
        tail = ref[HEAD:HEAD + 16, :].astype(F32)
        return tail[0:1], tail[1:2] + tail[2:3], ref[0:HEAD, :].astype(F32)

    def merge(parts):
        m = functools.reduce(jnp.maximum, [p[0] for p in parts])
        scales = [jnp.exp2(p[0] - m) for p in parts]
        l = functools.reduce(jnp.add, [p[1] * a for p, a in zip(parts, scales)])
        o = functools.reduce(jnp.add, [p[2] * a for p, a in zip(parts, scales)])
        return m, l, o

    def pair_copy(i):
        return remote(pair_out.at[i], pair_in.at[i], 4, pair_recv.at[i], dev(z, x, sib))

    def x_copy(i, d):
        return remote(x_out.at[i, d - 1], x_in.at[i, d - 1], 5, x_recv.at[i],
                      dev(z, (x + d) % nx, c))

    def z_copy(i):
        return remote(z_out.at[i], z_in.at[i], 6, z_recv.at[i], dev((z + far(i)) % nz, x, c))

    def stage_partials(i):
        z_ = (z + far(i)) % nz
        drain(queries.at[pl.ds(0, nx)], qc_recv.at[i])
        for d in range(nx):
            put(pair_out.at[i, d], *partial(dev(z_, (x + d) % nx, sib)))
        pair_copy(i).start()
        for d in range(nx):
            put(pair_own.at[i, d], *partial(dev(z_, (x + d) % nx, c)))

    def stage_x(i):
        pair_copy(i).wait_recv()
        for d in range(nx):
            merged = merge([get(pair_own.at[i, d]), get(pair_in.at[i, d])])
            if d == 0:
                put(x_own.at[i], *merged)
            else:
                put_half(x_out.at[i, d - 1], *merged)
                x_copy(i, d).start()

    def stage_z(i):
        drain(x_in.at[i], x_recv.at[i])
        merged = merge([get(x_own.at[i])] + [get_half(x_in.at[i, d]) for d in range(nx - 1)])

        @pl.when(i < nz - 1)
        def _():
            put_half(z_out.at[i], *merged)
            z_copy(i).start()

        @pl.when(i == nz - 1)
        def _():
            put(z_own, *merged)

    forward_x(0)

    def step(i, carry):
        @pl.when(i < nz - 1)
        def _():
            forward_x(i + 1)

        @pl.when(i < nz)
        def _():
            stage_partials(i)

        @pl.when(i >= 1)
        def _():
            stage_x(i - 1)

        @pl.when(i >= lag)
        def _():
            stage_z(i - lag)

        return carry

    lag = min(LAG, nz)
    lax.fori_loop(0, nz + 1, step, 0)

    s = owner_ref[me]
    turned = turn_queries(me, s)
    cosine, sine = step_turn(s)
    fresh = newk_ref[...].astype(F32)
    fresh = (fresh * cosine + pltpu.roll(fresh, HEAD // 2, 1) * sine).astype(BF16)
    scores = contract(fresh, turned, ((1,), (1,))) * score_scale
    row_step = lax.broadcasted_iota(jnp.int32, (steps, rows), 1) % steps
    causal = lax.broadcasted_iota(jnp.int32, (steps, rows), 0) <= row_step
    scores = jnp.where(causal, scores, NEG)
    m = shifted(jnp.max(scores, axis=0, keepdims=True))
    weights = jnp.where(causal, jnp.exp2(scores - m), 0.0)
    l = jnp.sum(weights, axis=0, keepdims=True)
    fresh = (m, l, contract(newv_ref[...], weights.astype(BF16), ((0,), (0,))))

    def trail(i, carry):
        stage_z(i)
        return carry

    lax.fori_loop(nz + 1 - lag, nz, trail, 0)
    parts = [fresh]
    for i in range(nz - 1):
        z_copy(i).wait_recv()
        parts.append(get_half(z_in.at[i]))
    parts.append(get(z_own))
    m, l, o = merge(parts)
    result = jnp.transpose(o / l).astype(BF16)
    for g in range(heads):
        out_ref[:, g * HEAD:(g + 1) * HEAD] = result[g * steps:(g + 1) * steps]

    for kind, ref in enumerate((
        counts.at[pl.ds(0, group - 1)], counts.at[pl.ds(0, (nz - 1) * group)], totals.at[pl.ds(0, ny - 1)],
        queries.at[pl.ds(0, seqs - 1)], pair_out, x_out, z_out,
    )):
        drain(ref, send_sem.at[kind])


def shards(
    nz, nx, ny,
    prompt_keys, prompt_values, keep_mask, owner_sequence, step_queries, new_keys, new_values,
):
    seqs = prompt_keys.shape[0]
    steps = step_queries.shape[1]
    freq = frequencies(HEAD // 2)
    freq = jnp.concatenate([freq, freq])[None]
    hbm = pl.BlockSpec(memory_space=pltpu.HBM)
    vmem = pl.BlockSpec(memory_space=pltpu.VMEM)
    dma = pltpu.SemaphoreType.DMA
    group = nx * 2
    out = pl.pallas_call(
        functools.partial(kernel, nz, nx, ny),
        out_shape=jax.ShapeDtypeStruct((steps, step_queries.shape[3]), BF16),
        in_specs=[hbm, hbm, vmem] + [hbm] * 5,
        out_specs=vmem,
        scratch_shapes=[
            pltpu.SMEM((seqs,), jnp.int32),
            pltpu.VMEM((2, 1, seqs), jnp.int32),
            pltpu.VMEM((steps, step_queries.shape[3]), BF16),
            pltpu.VMEM((steps, HEAD), BF16),
            pltpu.VMEM((steps, HEAD), BF16),
            pltpu.VMEM((seqs, 2 * BLOCK, HEAD), BF16),
            pltpu.VMEM((seqs, 2 * BLOCK, HEAD), BF16),
            pltpu.VMEM((seqs, HEAD, HEAD), BF16),
            pltpu.VMEM((seqs, 1, seqs), F32),
            pltpu.VMEM((ny, 1, seqs), F32),
            pltpu.VMEM((6, seqs, HEAD), F32),
            pltpu.VMEM((2, seqs, HEAD), F32),
            pltpu.VMEM((nz, nx, HEAD + 8, HEAD), F32),
            pltpu.VMEM((nz, nx, HEAD + 8, HEAD), F32),
            pltpu.VMEM((nz, nx, HEAD + 8, HEAD), F32),
            pltpu.VMEM((nz, nx - 1, HEAD + 16, HEAD), BF16),
            pltpu.VMEM((nz, nx - 1, HEAD + 16, HEAD), BF16),
            pltpu.VMEM((nz, HEAD + 8, HEAD), F32),
            pltpu.VMEM((nz - 1, HEAD + 16, HEAD), BF16),
            pltpu.VMEM((nz - 1, HEAD + 16, HEAD), BF16),
            pltpu.VMEM((HEAD + 8, HEAD), F32),
            dma((5,)), dma((5,)), dma((7,)), dma, dma, dma,
            dma((nz,)), dma((nz,)), dma((nz,)), dma((nz,)), dma((nz,)), dma((nz,)),
        ],
        compiler_params=pltpu.CompilerParams(
            collective_id=0, has_side_effects=True, vmem_limit_bytes=64 * 1024 * 1024
        ),
    )(
        owner_sequence, keep_mask.transpose(1, 2, 0), freq, step_queries[0, :, 0], new_keys[0],
        new_values[0],
        prompt_keys, prompt_values,
    )
    return out[None, :, None]


def solution(mesh):
    in_specs = (
        P(None, "seq", "tp"),
        P(None, "seq", "tp"),
        P(None, "seq", "tp"),
        P(),
        P("seq", None, "tp", None),
        P("seq", None, "tp"),
        P("seq", None, "tp"),
    )
    out_specs = P("seq", None, "tp", None)
    seq = mesh.shape["seq"]
    nx = 4 if seq >= 64 else 2
    body = functools.partial(shards, seq // (2 * nx), nx, mesh.shape["tp"])
    return jax.shard_map(body, mesh=mesh, in_specs=in_specs, out_specs=out_specs, check_vma=False)
```

```python
import functools
import math

import jax
import jax.numpy as jnp
from jax import lax
from jax.experimental import pallas as pl
from jax.experimental.pallas import tpu as pltpu
from jax.sharding import PartitionSpec as P

BLOCK = 128
HEAD = 128
NEG = -1e30
LAG = 4
MESH = pl.DeviceIdType.MESH
F32 = jnp.float32
BF16 = jnp.bfloat16


def frequencies(half_width):
    position_index = jnp.arange(half_width).astype(jnp.float32)
    base_rate = jnp.exp(position_index * (-2.0 / (2 * half_width)) * math.log(500000.0))
    wavelength = 2.0 * math.pi / base_rate
    smooth = (8192.0 / wavelength - 1.0) / 3.0
    blended = (1.0 - smooth) * base_rate / 8.0 + smooth * base_rate
    return jnp.where(
        wavelength < 2048.0, base_rate, jnp.where(wavelength > 8192.0, base_rate / 8.0, blended)
    )


def kernel(
    nz, nx, ny,
    owner_hbm, mask_hbm, freq_ref, query_hbm, newk_hbm, newv_hbm, keys_hbm, values_hbm,
    out_ref,
    owner_ref, mask_ref, query_ref, newk_ref, newv_ref,
    keys, values, queries, counts, totals, table, live, pair_out, pair_in, pair_own,
    x_out, x_in, x_own, z_out, z_in,
    load_sem, small_sem, send_sem, c1_recv, c2_recv, t_recv,
    qz_recv, qx_recv, qc_recv, pair_recv, x_recv, z_recv,
):
    seqs = nz * nx * 2
    group = nx * 2
    tokens = 2 * BLOCK
    steps = newk_ref.shape[0]
    heads = query_ref.shape[1] // HEAD
    rows = steps * heads
    score_scale = math.log2(math.e) / math.sqrt(HEAD)

    me = lax.axis_index("seq")
    tp = lax.axis_index("tp")
    z = me // group
    x = (me // 2) % nx
    c = me % 2
    sib = 1 - c

    def dev(z_, x_, c_):
        return (z_ * nx + x_) * 2 + c_

    def far(i):
        half = nz // 2
        return (half + (i % 2) * (nz - (i + 1) // 2) + (1 - i % 2) * (i // 2)) % nz

    def remote(ref, dst, send, recv, where, where_tp=None):
        return pltpu.make_async_remote_copy(
            src_ref=ref, dst_ref=dst, send_sem=send_sem.at[send], recv_sem=recv,
            device_id=(where, tp if where_tp is None else where_tp), device_id_type=MESH,
        )

    def drain(ref, sem):
        pltpu.make_async_copy(ref, ref, sem).wait()

    chunks = 4 if seqs > 8 else 2
    chunk = seqs // chunks

    def load(i):
        part = pl.ds(i * chunk, chunk)
        return pltpu.make_async_copy(keys_hbm.at[part], keys.at[part], load_sem.at[i])

    load_values = pltpu.make_async_copy(values_hbm, values, load_sem.at[chunks])
    small = [
        pltpu.make_async_copy(src, dst, small_sem.at[i])
        for i, (src, dst) in enumerate((
            (mask_hbm, mask_ref), (query_hbm, query_ref), (owner_hbm, owner_ref),
            (newk_hbm, newk_ref), (newv_hbm, newv_ref),
        ))
    ]
    for copy in small:
        copy.start()
    for i in range(chunks):
        load(i).start()
    load_values.start()

    small[0].wait()
    flags = [mask_ref[j].astype(F32) for j in range(2)]
    counts[me] = flags[0] + flags[1]
    small[1].wait()
    for g in range(heads):
        queries[me, g * steps:(g + 1) * steps, :] = query_ref[:, g * HEAD:(g + 1) * HEAD]

    barrier = pltpu.get_barrier_semaphore()
    near = z * group
    xc = x * 2 + c
    for r in range(1, group):
        pl.semaphore_signal(barrier, inc=1, device_id=(near + (xc + r) % group, tp), device_id_type=MESH)
    for d in range(1, nz):
        pl.semaphore_signal(barrier, inc=1, device_id=(dev((z + d) % nz, x, c), tp), device_id_type=MESH)
    for d in range(1, ny):
        pl.semaphore_signal(barrier, inc=1, device_id=(me, (tp + d) % ny), device_id_type=MESH)
    pl.semaphore_wait(barrier, group - 1 + nz - 1 + ny - 1)

    def counts_near(r):
        return remote(counts.at[me], counts.at[me], 0, c1_recv, near + (xc + r) % group)

    def counts_far(d):
        part = pl.ds(near, group)
        return remote(counts.at[part], counts.at[part], 1, c2_recv, dev((z + d) % nz, x, c))

    def totals_out(d):
        return remote(totals.at[tp], totals.at[tp], 2, t_recv, me, (tp + d) % ny)

    def query(slot, recv, where):
        return remote(queries.at[slot], queries.at[slot], 3, recv, where)

    def query_z(i):
        return query(me, qz_recv.at[i], dev((z - far(i) + nz) % nz, x, c))

    def query_z_in(i):
        slot = dev((z + far(i)) % nz, x, c)
        return query(slot, qz_recv.at[i], slot)

    def query_x(i, d):
        return query(dev((z + far(i)) % nz, x, c), qx_recv.at[i], dev(z, (x + d) % nx, c))

    def query_c(i, d):
        slot = dev((z + far(i)) % nz, (x - d + nx) % nx, c)
        return query(slot, qc_recv.at[i], dev(z, x, sib))

    def forward_z(i):
        for d in range(1, nx):
            query_x(i, d).start()
        query_c(i, 0).start()

    def forward_x(i):
        drain(queries.at[pl.ds(0, nx - 1)], qx_recv.at[i])
        for d in range(1, nx):
            query_c(i, d).start()

    for r in range(1, group):
        counts_near(r).start()
    for i in range(nz - 1):
        query_z(i).start()
    forward_z(nz - 1)
    drain(counts.at[pl.ds(0, group - 1)], c1_recv)
    for d in range(1, nz):
        counts_far(d).start()
    for i in range(nz - 1):
        query_z_in(i).wait_recv()
        forward_z(i)
    drain(counts.at[pl.ds(0, (nz - 1) * group)], c2_recv)

    before = jnp.zeros((1, seqs), F32)
    total = jnp.zeros((1, seqs), F32)
    for j in range(seqs):
        row = counts[j]
        total = total + row
        before = before + jnp.where(j < me, row, 0.0)
    totals[tp] = total
    for d in range(1, ny):
        totals_out(d).start()

    freq = freq_ref[...]
    lane = lax.broadcasted_iota(jnp.int32, (1, HEAD), 1)
    sign = jnp.where(lane < HEAD // 2, -1.0, 1.0).astype(F32)

    def down(row):
        return jnp.transpose(jnp.broadcast_to(row, (HEAD, seqs)))

    slot0 = before
    slot1 = before + flags[0]
    first_block = (2 * me).astype(F32)
    for j, slot in enumerate((slot0, slot1)):
        angle = (down(slot) - (first_block + j)) * float(BLOCK) * freq
        table[2 * j] = jnp.cos(angle)
        table[2 * j + 1] = jnp.sin(angle) * sign
        live[j] = down(flags[j])

    def rotate_keys(k, carry):
        for i, j in ((2 * k, 0), (2 * k, 1), (2 * k + 1, 0), (2 * k + 1, 1)):
            cosine = table[2 * j, pl.ds(i, 1), :]
            sine = table[2 * j + 1, pl.ds(i, 1), :]
            part = pl.ds(j * BLOCK, BLOCK)
            packed = keys[i, part, :]
            swapped = pltpu.roll(packed, HEAD // 2, 1).astype(F32)
            turned = packed.astype(F32) * cosine + swapped * sine
            keys[i, part, :] = turned.astype(BF16)
        return carry

    for i in range(chunks):
        load(i).wait()
        lax.fori_loop(i * chunk // 2, (i + 1) * chunk // 2, rotate_keys, 0)
    load_values.wait()

    for copy in small[2:]:
        copy.wait()

    longest = total
    drain(totals.at[pl.ds(0, ny - 1)], t_recv)
    for d in range(1, ny):
        longest = jnp.maximum(longest, totals[(tp + d) % ny])
    angle = down(longest) * float(BLOCK) * freq
    table[4] = jnp.cos(angle)
    table[5] = jnp.sin(angle)
    step_angle = lax.broadcasted_iota(jnp.int32, (steps, HEAD), 0).astype(F32) * freq
    step_cos = jnp.cos(step_angle)
    step_sin = jnp.sin(step_angle)

    def step_turn(s):
        cosine = table[4, pl.ds(s, 1), :]
        sine = table[5, pl.ds(s, 1), :]
        return (
            cosine * step_cos - sine * step_sin,
            (sine * step_cos + cosine * step_sin) * sign,
        )

    def turn_queries(slot, s):
        cosine, sine = step_turn(s)
        stored = queries[slot].astype(F32)
        swapped = pltpu.roll(stored, HEAD // 2, 1)
        shape = (heads, steps, HEAD)
        turned = stored.reshape(shape) * cosine[None] + swapped.reshape(shape) * sine[None]
        return turned.reshape(rows, HEAD).astype(BF16)

    def contract(a, b, dims):
        return lax.dot_general(a, b, (dims, ((), ())), preferred_element_type=F32)

    def shifted(m):
        return m.astype(BF16).astype(F32)

    def partials(slots):
        places = [owner_ref[slot] for slot in slots]
        turned = [turn_queries(slot, s) for slot, s in zip(slots, places)]
        scores = [contract(keys[s], q, ((1,), (1,))) * score_scale for s, q in zip(places, turned)]
        kept = [[live[j, pl.ds(s, 1), :] > 0.5 for j in range(2)] for s in places]
        pieces = [[a[j * BLOCK:(j + 1) * BLOCK] for j in range(2)] for a in scores]
        tops = [
            [jnp.where(k[j], jnp.max(a[j], axis=0, keepdims=True), NEG) for j in range(2)]
            for k, a in zip(kept, pieces)
        ]
        m = [shifted(jnp.maximum(*t)) for t in tops]
        weights = [
            [jnp.exp2(a[j] - jnp.where(k[j], b, -NEG)) for j in range(2)]
            for k, a, b in zip(kept, pieces, m)
        ]
        l = [jnp.sum(w[0] + w[1], axis=0, keepdims=True) for w in weights]
        o = [
            contract(values[s], jnp.concatenate(w, axis=0).astype(BF16), ((0,), (0,)))
            for s, w in zip(places, weights)
        ]
        return list(zip(m, l, o))

    sub8 = lax.broadcasted_iota(jnp.int32, (8, HEAD), 0)

    def put(ref, m, l, o):
        ref[0:HEAD, :] = o
        ref[HEAD:HEAD + 8, :] = jnp.where(sub8 == 0, m, l)

    def get(ref):
        return ref[HEAD:HEAD + 1, :], ref[HEAD + 1:HEAD + 2, :], ref[0:HEAD, :]

    def put_half(ref, m, l, o):
        high = l.astype(BF16).astype(F32)
        ref[0:HEAD, :] = o.astype(BF16)
        tail = jnp.where(sub8 == 0, m, jnp.where(sub8 == 1, high, l - high))
        ref[HEAD:HEAD + 8, :] = tail.astype(BF16)

    def get_half(ref):
        tail = ref[HEAD:HEAD + 8, :].astype(F32)
        return tail[0:1], tail[1:2] + tail[2:3], ref[0:HEAD, :].astype(F32)

    def merge(parts):
        m = functools.reduce(jnp.maximum, [p[0] for p in parts])
        scales = [jnp.exp2(p[0] - m) for p in parts]
        l = functools.reduce(jnp.add, [p[1] * a for p, a in zip(parts, scales)])
        o = functools.reduce(jnp.add, [p[2] * a for p, a in zip(parts, scales)])
        return m, l, o

    def pair_copy(i):
        return remote(pair_out.at[i], pair_in.at[i], 4, pair_recv.at[i], dev(z, x, sib))

    def x_copy(i, d):
        return remote(x_out.at[i, d - 1], x_in.at[i, d - 1], 5, x_recv.at[i],
                      dev(z, (x + d) % nx, c))

    def z_copy(i):
        return remote(z_out.at[i], z_in.at[i], 6, z_recv.at[i], dev((z + far(i)) % nz, x, c))

    def stage_partials(i):
        z_ = (z + far(i)) % nz
        drain(queries.at[pl.ds(0, nx)], qc_recv.at[i])
        for d, part in enumerate(partials([dev(z_, (x + d) % nx, sib) for d in range(nx)])):
            put(pair_out.at[i, d], *part)
        pair_copy(i).start()
        for d, part in enumerate(partials([dev(z_, (x + d) % nx, c) for d in range(nx)])):
            put(pair_own.at[i, d], *part)

    def stage_x(i):
        pair_copy(i).wait_recv()
        for d in range(nx):
            merged = merge([get(pair_own.at[i, d]), get(pair_in.at[i, d])])
            if d == 0:
                put(x_own.at[i], *merged)
            else:
                put_half(x_out.at[i, d - 1], *merged)
                x_copy(i, d).start()

    def stage_z(i):
        drain(x_in.at[i], x_recv.at[i])
        return merge([get(x_own.at[i])] + [get_half(x_in.at[i, d]) for d in range(nx - 1)])

    def send_z(i):
        put_half(z_out.at[i], *stage_z(i))
        z_copy(i).start()

    forward_x(0)

    def step(i, carry):
        @pl.when(i < nz - 1)
        def _():
            forward_x(i + 1)

        @pl.when(i < nz)
        def _():
            stage_partials(i)

        @pl.when(i >= 1)
        def _():
            stage_x(i - 1)

        @pl.when((i >= lag) & (i - lag < nz - 1))
        def _():
            send_z(i - lag)

        return carry

    lag = min(LAG, nz)
    lax.fori_loop(0, nz + 1, step, 0)

    s = owner_ref[me]
    turned = turn_queries(me, s)
    cosine, sine = step_turn(s)
    fresh = newk_ref[...].astype(F32)
    fresh = (fresh * cosine + pltpu.roll(fresh, HEAD // 2, 1) * sine).astype(BF16)
    scores = contract(fresh, turned, ((1,), (1,))) * score_scale
    row_step = lax.broadcasted_iota(jnp.int32, (steps, rows), 1) % steps
    causal = lax.broadcasted_iota(jnp.int32, (steps, rows), 0) <= row_step
    scores = jnp.where(causal, scores, NEG)
    m = shifted(jnp.max(scores, axis=0, keepdims=True))
    weights = jnp.where(causal, jnp.exp2(scores - m), 0.0)
    l = jnp.sum(weights, axis=0, keepdims=True)
    fresh = (m, l, contract(newv_ref[...], weights.astype(BF16), ((0,), (0,))))

    for i in range(nz + 1 - lag, nz - 1):
        send_z(i)
    parts = [fresh]
    parts.append(stage_z(nz - 1))
    for i in range(nz-1):
        z_copy(i).wait_recv()
        parts.append(get_half(z_in.at[i]))
    m, l, o = merge(parts)
    result = jnp.transpose(o / l).astype(BF16)
    for g in range(heads):
        out_ref[:, g * HEAD:(g + 1) * HEAD] = result[g * steps:(g + 1) * steps]

    for kind, ref in enumerate((
        counts.at[pl.ds(0, group - 1)], counts.at[pl.ds(0, (nz - 1) * group)], totals.at[pl.ds(0, ny - 1)],
        queries.at[pl.ds(0, seqs - 1)], pair_out, x_out, z_out,
    )):
        drain(ref, send_sem.at[kind])


def shards(
    nz, nx, ny,
    prompt_keys, prompt_values, keep_mask, owner_sequence, step_queries, new_keys, new_values,
):
    seqs = prompt_keys.shape[0]
    steps = step_queries.shape[1]
    freq = frequencies(HEAD // 2)
    freq = jnp.concatenate([freq, freq])[None]
    hbm = pl.BlockSpec(memory_space=pltpu.HBM)
    vmem = pl.BlockSpec(memory_space=pltpu.VMEM)
    dma = pltpu.SemaphoreType.DMA
    group = nx * 2
    out = pl.pallas_call(
        functools.partial(kernel, nz, nx, ny),
        out_shape=jax.ShapeDtypeStruct((steps, step_queries.shape[3]), BF16),
        in_specs=[hbm, hbm, vmem] + [hbm] * 5,
        out_specs=vmem,
        scratch_shapes=[
            pltpu.SMEM((seqs,), jnp.int32),
            pltpu.VMEM((2, 1, seqs), jnp.int32),
            pltpu.VMEM((steps, step_queries.shape[3]), BF16),
            pltpu.VMEM((steps, HEAD), BF16),
            pltpu.VMEM((steps, HEAD), BF16),
            pltpu.VMEM((seqs, 2 * BLOCK, HEAD), BF16),
            pltpu.VMEM((seqs, 2 * BLOCK, HEAD), BF16),
            pltpu.VMEM((seqs, HEAD, HEAD), BF16),
            pltpu.VMEM((seqs, 1, seqs), F32),
            pltpu.VMEM((ny, 1, seqs), F32),
            pltpu.VMEM((6, seqs, HEAD), F32),
            pltpu.VMEM((2, seqs, HEAD), F32),
            pltpu.VMEM((nz, nx, HEAD + 8, HEAD), F32),
            pltpu.VMEM((nz, nx, HEAD + 8, HEAD), F32),
            pltpu.VMEM((nz, nx, HEAD + 8, HEAD), F32),
            pltpu.VMEM((nz, nx - 1, HEAD + 8, HEAD), BF16),
            pltpu.VMEM((nz, nx - 1, HEAD + 8, HEAD), BF16),
            pltpu.VMEM((nz, HEAD + 8, HEAD), F32),
            pltpu.VMEM((nz - 1, HEAD + 8, HEAD), BF16),
            pltpu.VMEM((nz - 1, HEAD + 8, HEAD), BF16),
            dma((5,)), dma((5,)), dma((7,)), dma, dma, dma,
            dma((nz,)), dma((nz,)), dma((nz,)), dma((nz,)), dma((nz,)), dma((nz,)),
        ],
        compiler_params=pltpu.CompilerParams(
            collective_id=0, has_side_effects=True, vmem_limit_bytes=64 * 1024 * 1024
        ),
    )(
        owner_sequence, keep_mask.transpose(1, 2, 0), freq, step_queries[0, :, 0], new_keys[0],
        new_values[0],
        prompt_keys, prompt_values,
    )
    return out[None, :, None]


def solution(mesh):
    in_specs = (
        P(None, "seq", "tp"),
        P(None, "seq", "tp"),
        P(None, "seq", "tp"),
        P(),
        P("seq", None, "tp", None),
        P("seq", None, "tp"),
        P("seq", None, "tp"),
    )
    out_specs = P("seq", None, "tp", None)
    seq = mesh.shape["seq"]
    nx = 4 if seq >= 64 else 2
    body = functools.partial(shards, seq // (2 * nx), nx, mesh.shape["tp"])
    return jax.shard_map(body, mesh=mesh, in_specs=in_specs, out_specs=out_specs, check_vma=False)
```

```python
import functools
import math

import jax
import jax.numpy as jnp
from jax import lax
from jax.experimental import pallas as pl
from jax.experimental.pallas import tpu as pltpu
from jax.sharding import PartitionSpec as P

BLOCK = 128
HEAD = 128
NEG = -1e30
LAG = 4
MESH = pl.DeviceIdType.MESH
F32 = jnp.float32
BF16 = jnp.bfloat16


def frequencies(half_width):
    position_index = jnp.arange(half_width).astype(jnp.float32)
    base_rate = jnp.exp(position_index * (-2.0 / (2 * half_width)) * math.log(500000.0))
    wavelength = 2.0 * math.pi / base_rate
    smooth = (8192.0 / wavelength - 1.0) / 3.0
    blended = (1.0 - smooth) * base_rate / 8.0 + smooth * base_rate
    return jnp.where(
        wavelength < 2048.0, base_rate, jnp.where(wavelength > 8192.0, base_rate / 8.0, blended)
    )


def kernel(
    nz, nx, ny,
    owner_hbm, mask_hbm, freq_ref, query_hbm, newk_hbm, newv_hbm, keys_hbm, values_hbm,
    out_ref,
    owner_ref, mask_ref, query_ref, newk_ref, newv_ref,
    keys, values, queries, counts, totals, table, live, pair_out, pair_in, pair_own,
    x_out, x_in, x_own, z_out, z_in,
    load_sem, small_sem, send_sem, c1_recv, c2_recv, t_recv,
    qz_recv, qx_recv, qc_recv, pair_recv, x_recv, z_recv,
):
    seqs = nz * nx * 2
    group = nx * 2
    tokens = 2 * BLOCK
    steps = newk_ref.shape[0]
    heads = query_ref.shape[1] // HEAD
    rows = steps * heads
    score_scale = math.log2(math.e) / math.sqrt(HEAD)

    me = lax.axis_index("seq")
    tp = lax.axis_index("tp")
    z = me // group
    x = (me // 2) % nx
    c = me % 2
    sib = 1 - c

    def dev(z_, x_, c_):
        return (z_ * nx + x_) * 2 + c_

    def far(i):
        half = nz // 2
        return (half + (i % 2) * (nz - (i + 1) // 2) + (1 - i % 2) * (i // 2)) % nz

    def remote(ref, dst, send, recv, where, where_tp=None):
        return pltpu.make_async_remote_copy(
            src_ref=ref, dst_ref=dst, send_sem=send_sem.at[send], recv_sem=recv,
            device_id=(where, tp if where_tp is None else where_tp), device_id_type=MESH,
        )

    def drain(ref, sem):
        pltpu.make_async_copy(ref, ref, sem).wait()

    chunks = 4 if seqs > 8 else 2
    chunk = seqs // chunks

    def load(i):
        part = pl.ds(i * chunk, chunk)
        return pltpu.make_async_copy(keys_hbm.at[part], keys.at[part], load_sem.at[i])

    load_values = pltpu.make_async_copy(values_hbm, values, load_sem.at[chunks])
    small = [
        pltpu.make_async_copy(src, dst, small_sem.at[i])
        for i, (src, dst) in enumerate((
            (mask_hbm, mask_ref), (query_hbm, query_ref), (owner_hbm, owner_ref),
            (newk_hbm, newk_ref), (newv_hbm, newv_ref),
        ))
    ]
    for copy in small:
        copy.start()
    for i in range(chunks):
        load(i).start()
    load_values.start()

    small[0].wait()
    flags = [mask_ref[j].astype(F32) for j in range(2)]
    counts[me] = flags[0] + flags[1]
    small[1].wait()
    for g in range(heads):
        queries[me, g * steps:(g + 1) * steps, :] = query_ref[:, g * HEAD:(g + 1) * HEAD]

    barrier = pltpu.get_barrier_semaphore()
    near = z * group
    xc = x * 2 + c
    for r in range(1, group):
        pl.semaphore_signal(barrier, inc=1, device_id=(near + (xc + r) % group, tp), device_id_type=MESH)
    for d in range(1, nz):
        pl.semaphore_signal(barrier, inc=1, device_id=(dev((z + d) % nz, x, c), tp), device_id_type=MESH)
    for d in range(1, ny):
        pl.semaphore_signal(barrier, inc=1, device_id=(me, (tp + d) % ny), device_id_type=MESH)
    pl.semaphore_wait(barrier, group - 1 + nz - 1 + ny - 1)

    def counts_near(r):
        return remote(counts.at[me], counts.at[me], 0, c1_recv, near + (xc + r) % group)

    def counts_far(d):
        part = pl.ds(near, group)
        return remote(counts.at[part], counts.at[part], 1, c2_recv, dev((z + d) % nz, x, c))

    def totals_out(d):
        return remote(totals.at[tp], totals.at[tp], 2, t_recv, me, (tp + d) % ny)

    def query(slot, recv, where):
        return remote(queries.at[slot], queries.at[slot], 3, recv, where)

    def query_z(i):
        return query(me, qz_recv.at[i], dev((z - far(i) + nz) % nz, x, c))

    def query_z_in(i):
        slot = dev((z + far(i)) % nz, x, c)
        return query(slot, qz_recv.at[i], slot)

    def query_x(i, d):
        return query(dev((z + far(i)) % nz, x, c), qx_recv.at[i], dev(z, (x + d) % nx, c))

    def query_c(i, d):
        slot = dev((z + far(i)) % nz, (x - d + nx) % nx, c)
        return query(slot, qc_recv.at[i], dev(z, x, sib))

    def forward_z(i):
        for d in range(1, nx):
            query_x(i, d).start()
        query_c(i, 0).start()

    def forward_x(i):
        drain(queries.at[pl.ds(0, nx - 1)], qx_recv.at[i])
        for d in range(1, nx):
            query_c(i, d).start()

    for r in range(1, group):
        counts_near(r).start()
    for i in range(nz - 1):
        query_z(i).start()
    forward_z(nz - 1)
    drain(counts.at[pl.ds(0, group - 1)], c1_recv)
    for d in range(1, nz):
        counts_far(d).start()
    for i in range(nz - 1):
        query_z_in(i).wait_recv()
        forward_z(i)
    drain(counts.at[pl.ds(0, (nz - 1) * group)], c2_recv)

    before = jnp.zeros((1, seqs), F32)
    total = jnp.zeros((1, seqs), F32)
    for j in range(seqs):
        row = counts[j]
        total = total + row
        before = before + jnp.where(j < me, row, 0.0)
    totals[tp] = total
    for d in range(1, ny):
        totals_out(d).start()

    freq = freq_ref[...]
    lane = lax.broadcasted_iota(jnp.int32, (1, HEAD), 1)
    sign = jnp.where(lane < HEAD // 2, -1.0, 1.0).astype(F32)

    def down(row):
        return jnp.transpose(jnp.broadcast_to(row, (HEAD, seqs)))

    slot0 = before
    slot1 = before + flags[0]
    first_block = (2 * me).astype(F32)
    for j, slot in enumerate((slot0, slot1)):
        angle = (down(slot) - (first_block + j)) * float(BLOCK) * freq
        table[2 * j] = jnp.cos(angle)
        table[2 * j + 1] = jnp.sin(angle) * sign
        live[j] = down(flags[j])

    def rotate_keys(k, carry):
        for i, j in ((2 * k, 0), (2 * k, 1), (2 * k + 1, 0), (2 * k + 1, 1)):
            cosine = table[2 * j, pl.ds(i, 1), :]
            sine = table[2 * j + 1, pl.ds(i, 1), :]
            part = pl.ds(j * BLOCK, BLOCK)
            packed = keys[i, part, :]
            swapped = pltpu.roll(packed, HEAD // 2, 1).astype(F32)
            turned = packed.astype(F32) * cosine + swapped * sine
            keys[i, part, :] = turned.astype(BF16)
        return carry

    for i in range(chunks):
        load(i).wait()
        lax.fori_loop(i * chunk // 2, (i + 1) * chunk // 2, rotate_keys, 0)
    load_values.wait()

    for copy in small[2:]:
        copy.wait()

    longest = total
    drain(totals.at[pl.ds(0, ny - 1)], t_recv)
    for d in range(1, ny):
        longest = jnp.maximum(longest, totals[(tp + d) % ny])
    angle = down(longest) * float(BLOCK) * freq
    table[4] = jnp.cos(angle)
    table[5] = jnp.sin(angle)
    step_angle = lax.broadcasted_iota(jnp.int32, (steps, HEAD), 0).astype(F32) * freq
    step_cos = jnp.cos(step_angle)
    step_sin = jnp.sin(step_angle)

    def step_turn(s):
        cosine = table[4, pl.ds(s, 1), :]
        sine = table[5, pl.ds(s, 1), :]
        return (
            cosine * step_cos - sine * step_sin,
            (sine * step_cos + cosine * step_sin) * sign,
        )

    def turn_queries(slot, s):
        cosine, sine = step_turn(s)
        stored = queries[slot].astype(F32)
        swapped = pltpu.roll(stored, HEAD // 2, 1)
        shape = (heads, steps, HEAD)
        turned = stored.reshape(shape) * cosine[None] + swapped.reshape(shape) * sine[None]
        return turned.reshape(rows, HEAD).astype(BF16)

    def contract(a, b, dims):
        return lax.dot_general(a, b, (dims, ((), ())), preferred_element_type=F32)

    def shifted(m):
        return m.astype(BF16).astype(F32)

    def partials(slots):
        places = [owner_ref[slot] for slot in slots]
        turned = [turn_queries(slot, s) for slot, s in zip(slots, places)]
        scores = [contract(keys[s], q, ((1,), (1,))) * score_scale for s, q in zip(places, turned)]
        kept = [[live[j, pl.ds(s, 1), :] > 0.5 for j in range(2)] for s in places]
        pieces = [[a[j * BLOCK:(j + 1) * BLOCK] for j in range(2)] for a in scores]
        tops = [
            [jnp.where(k[j], jnp.max(a[j], axis=0, keepdims=True), NEG) for j in range(2)]
            for k, a in zip(kept, pieces)
        ]
        m = [shifted(jnp.maximum(*t)) for t in tops]
        weights = [
            [jnp.exp2(a[j] - jnp.where(k[j], b, -NEG)) for j in range(2)]
            for k, a, b in zip(kept, pieces, m)
        ]
        l = [jnp.sum(w[0] + w[1], axis=0, keepdims=True) for w in weights]
        o = [
            contract(values[s], jnp.concatenate(w, axis=0).astype(BF16), ((0,), (0,)))
            for s, w in zip(places, weights)
        ]
        return list(zip(m, l, o))

    sub8 = lax.broadcasted_iota(jnp.int32, (8, HEAD), 0)

    def put(ref, m, l, o):
        ref[0:HEAD, :] = o
        ref[HEAD:HEAD + 8, :] = jnp.where(sub8 == 0, m, l)

    def get(ref):
        return ref[HEAD:HEAD + 1, :], ref[HEAD + 1:HEAD + 2, :], ref[0:HEAD, :]

    def put_half(ref, m, l, o):
        high = l.astype(BF16).astype(F32)
        ref[0:HEAD, :] = o.astype(BF16)
        tail = jnp.where(sub8 == 0, m, jnp.where(sub8 == 1, high, l - high))
        ref[HEAD:HEAD + 8, :] = tail.astype(BF16)

    def get_half(ref):
        tail = ref[HEAD:HEAD + 8, :].astype(F32)
        return tail[0:1], tail[1:2] + tail[2:3], ref[0:HEAD, :].astype(F32)

    def merge(parts):
        m = functools.reduce(jnp.maximum, [p[0] for p in parts])
        scales = [jnp.exp2(p[0] - m) for p in parts]
        l = functools.reduce(jnp.add, [p[1] * a for p, a in zip(parts, scales)])
        o = functools.reduce(jnp.add, [p[2] * a for p, a in zip(parts, scales)])
        return m, l, o

    def pair_copy(i):
        return remote(pair_out.at[i], pair_in.at[i], 4, pair_recv.at[i], dev(z, x, sib))

    def x_copy(i, d):
        return remote(x_out.at[i, d - 1], x_in.at[i, d - 1], 5, x_recv.at[i],
                      dev(z, (x + d) % nx, c))

    def z_copy(i):
        return remote(z_out.at[i], z_in.at[i], 6, z_recv.at[i], dev((z + far(i)) % nz, x, c))

    def stage_partials(i):
        z_ = (z + far(i)) % nz
        drain(queries.at[pl.ds(0, nx)], qc_recv.at[i])
        for d, part in enumerate(partials([dev(z_, (x + d) % nx, sib) for d in range(nx)])):
            put(pair_out.at[i, d], *part)
        pair_copy(i).start()

        @pl.when(i >= 1)
        def _():
            stage_x(i - 1)

        for d, part in enumerate(partials([dev(z_, (x + d) % nx, c) for d in range(nx)])):
            put(pair_own.at[i, d], *part)

    def stage_x(i):
        pair_copy(i).wait_recv()
        for d in range(nx):
            merged = merge([get(pair_own.at[i, d]), get(pair_in.at[i, d])])
            if d == 0:
                put(x_own.at[i], *merged)
            else:
                put_half(x_out.at[i, d - 1], *merged)
                x_copy(i, d).start()

    def stage_z(i):
        drain(x_in.at[i], x_recv.at[i])
        return merge([get(x_own.at[i])] + [get_half(x_in.at[i, d]) for d in range(nx - 1)])

    def send_z(i):
        put_half(z_out.at[i], *stage_z(i))
        z_copy(i).start()

    forward_x(0)
    forward_x(1)

    def step(i, carry):
        @pl.when(i < nz - 2)
        def _():
            forward_x(i + 2)

        @pl.when(i < nz)
        def _():
            stage_partials(i)

        @pl.when(i == nz)
        def _():
            stage_x(i - 1)

        @pl.when((i >= lag) & (i - lag < nz - 1))
        def _():
            send_z(i - lag)

        return carry

    lag = min(LAG, nz)
    lax.fori_loop(0, nz + 1, step, 0)

    s = owner_ref[me]
    turned = turn_queries(me, s)
    cosine, sine = step_turn(s)
    fresh = newk_ref[...].astype(F32)
    fresh = (fresh * cosine + pltpu.roll(fresh, HEAD // 2, 1) * sine).astype(BF16)
    scores = contract(fresh, turned, ((1,), (1,))) * score_scale
    row_step = lax.broadcasted_iota(jnp.int32, (steps, rows), 1) % steps
    causal = lax.broadcasted_iota(jnp.int32, (steps, rows), 0) <= row_step
    scores = jnp.where(causal, scores, NEG)
    m = shifted(jnp.max(scores, axis=0, keepdims=True))
    weights = jnp.where(causal, jnp.exp2(scores - m), 0.0)
    l = jnp.sum(weights, axis=0, keepdims=True)
    fresh = (m, l, contract(newv_ref[...], weights.astype(BF16), ((0,), (0,))))

    for i in range(nz + 1 - lag, nz - 1):
        send_z(i)
    parts = [fresh]
    parts.append(stage_z(nz - 1))
    for i in range(nz-1):
        z_copy(i).wait_recv()
        parts.append(get_half(z_in.at[i]))
    m, l, o = merge(parts)
    result = jnp.transpose(o / l).astype(BF16)
    for g in range(heads):
        out_ref[:, g * HEAD:(g + 1) * HEAD] = result[g * steps:(g + 1) * steps]

    for kind, ref in enumerate((
        counts.at[pl.ds(0, group - 1)], counts.at[pl.ds(0, (nz - 1) * group)], totals.at[pl.ds(0, ny - 1)],
        queries.at[pl.ds(0, seqs - 1)], pair_out, x_out, z_out,
    )):
        drain(ref, send_sem.at[kind])


def shards(
    nz, nx, ny,
    prompt_keys, prompt_values, keep_mask, owner_sequence, step_queries, new_keys, new_values,
):
    seqs = prompt_keys.shape[0]
    steps = step_queries.shape[1]
    freq = frequencies(HEAD // 2)
    freq = jnp.concatenate([freq, freq])[None]
    hbm = pl.BlockSpec(memory_space=pltpu.HBM)
    vmem = pl.BlockSpec(memory_space=pltpu.VMEM)
    dma = pltpu.SemaphoreType.DMA
    group = nx * 2
    out = pl.pallas_call(
        functools.partial(kernel, nz, nx, ny),
        out_shape=jax.ShapeDtypeStruct((steps, step_queries.shape[3]), BF16),
        in_specs=[hbm, hbm, vmem] + [hbm] * 5,
        out_specs=vmem,
        scratch_shapes=[
            pltpu.SMEM((seqs,), jnp.int32),
            pltpu.VMEM((2, 1, seqs), jnp.int32),
            pltpu.VMEM((steps, step_queries.shape[3]), BF16),
            pltpu.VMEM((steps, HEAD), BF16),
            pltpu.VMEM((steps, HEAD), BF16),
            pltpu.VMEM((seqs, 2 * BLOCK, HEAD), BF16),
            pltpu.VMEM((seqs, 2 * BLOCK, HEAD), BF16),
            pltpu.VMEM((seqs, HEAD, HEAD), BF16),
            pltpu.VMEM((seqs, 1, seqs), F32),
            pltpu.VMEM((ny, 1, seqs), F32),
            pltpu.VMEM((6, seqs, HEAD), F32),
            pltpu.VMEM((2, seqs, HEAD), F32),
            pltpu.VMEM((nz, nx, HEAD + 8, HEAD), F32),
            pltpu.VMEM((nz, nx, HEAD + 8, HEAD), F32),
            pltpu.VMEM((nz, nx, HEAD + 8, HEAD), F32),
            pltpu.VMEM((nz, nx - 1, HEAD + 8, HEAD), BF16),
            pltpu.VMEM((nz, nx - 1, HEAD + 8, HEAD), BF16),
            pltpu.VMEM((nz, HEAD + 8, HEAD), F32),
            pltpu.VMEM((nz - 1, HEAD + 8, HEAD), BF16),
            pltpu.VMEM((nz - 1, HEAD + 8, HEAD), BF16),
            dma((5,)), dma((5,)), dma((7,)), dma, dma, dma,
            dma((nz,)), dma((nz,)), dma((nz,)), dma((nz,)), dma((nz,)), dma((nz,)),
        ],
        compiler_params=pltpu.CompilerParams(
            collective_id=0, has_side_effects=True, vmem_limit_bytes=64 * 1024 * 1024
        ),
    )(
        owner_sequence, keep_mask.transpose(1, 2, 0), freq, step_queries[0, :, 0], new_keys[0],
        new_values[0],
        prompt_keys, prompt_values,
    )
    return out[None, :, None]


def solution(mesh):
    in_specs = (
        P(None, "seq", "tp"),
        P(None, "seq", "tp"),
        P(None, "seq", "tp"),
        P(),
        P("seq", None, "tp", None),
        P("seq", None, "tp"),
        P("seq", None, "tp"),
    )
    out_specs = P("seq", None, "tp", None)
    seq = mesh.shape["seq"]
    nx = 4 if seq >= 64 else 2
    body = functools.partial(shards, seq // (2 * nx), nx, mesh.shape["tp"])
    return jax.shard_map(body, mesh=mesh, in_specs=in_specs, out_specs=out_specs, check_vma=False)
```

```python
import functools
import math

import jax
import jax.numpy as jnp
from jax import lax
from jax.experimental import pallas as pl
from jax.experimental.pallas import tpu as pltpu
from jax.sharding import PartitionSpec as P

BLOCK = 128
HEAD = 128
NEG = -1e30
LAG = 4
MESH = pl.DeviceIdType.MESH
F32 = jnp.float32
BF16 = jnp.bfloat16


def frequencies(half_width):
    position_index = jnp.arange(half_width).astype(jnp.float32)
    base_rate = jnp.exp(position_index * (-2.0 / (2 * half_width)) * math.log(500000.0))
    wavelength = 2.0 * math.pi / base_rate
    smooth = (8192.0 / wavelength - 1.0) / 3.0
    blended = (1.0 - smooth) * base_rate / 8.0 + smooth * base_rate
    return jnp.where(
        wavelength < 2048.0, base_rate, jnp.where(wavelength > 8192.0, base_rate / 8.0, blended)
    )


def kernel(
    nz, nx, ny,
    owner_hbm, mask_hbm, freq_ref, query_hbm, newk_hbm, newv_hbm, keys_hbm, values_hbm,
    out_ref,
    owner_ref, mask_ref, query_ref, newk_ref, newv_ref,
    keys, values, queries, counts, totals, table, live, pair_out, pair_in, pair_own,
    x_out, x_in, x_own, z_out, z_in,
    load_sem, small_sem, send_sem, c1_recv, c2_recv, t_recv,
    qz_recv, qx_recv, qc_recv, pair_recv, x_recv, z_recv,
):
    seqs = nz * nx * 2
    group = nx * 2
    tokens = 2 * BLOCK
    steps = newk_ref.shape[0]
    heads = query_ref.shape[1] // HEAD
    rows = steps * heads
    score_scale = math.log2(math.e) / math.sqrt(HEAD)

    me = lax.axis_index("seq")
    tp = lax.axis_index("tp")
    z = me // group
    x = (me // 2) % nx
    c = me % 2
    sib = 1 - c

    def dev(z_, x_, c_):
        return (z_ * nx + x_) * 2 + c_

    def far(i):
        half = nz // 2
        return (half + (i % 2) * (nz - (i + 1) // 2) + (1 - i % 2) * (i // 2)) % nz

    def remote(ref, dst, send, recv, where, where_tp=None):
        return pltpu.make_async_remote_copy(
            src_ref=ref, dst_ref=dst, send_sem=send_sem.at[send], recv_sem=recv,
            device_id=(where, tp if where_tp is None else where_tp), device_id_type=MESH,
        )

    def drain(ref, sem):
        pltpu.make_async_copy(ref, ref, sem).wait()

    chunks = 4 if seqs > 8 else 2
    chunk = seqs // chunks

    def load(i):
        part = pl.ds(i * chunk, chunk)
        return pltpu.make_async_copy(keys_hbm.at[part], keys.at[part], load_sem.at[i])

    load_values = pltpu.make_async_copy(values_hbm, values, load_sem.at[chunks])
    small = [
        pltpu.make_async_copy(src, dst, small_sem.at[i])
        for i, (src, dst) in enumerate((
            (mask_hbm, mask_ref), (query_hbm, query_ref), (owner_hbm, owner_ref),
            (newk_hbm, newk_ref), (newv_hbm, newv_ref),
        ))
    ]
    for copy in small:
        copy.start()
    for i in range(chunks):
        load(i).start()
    load_values.start()

    small[0].wait()
    flags = [mask_ref[j].astype(F32) for j in range(2)]
    counts[me] = flags[0] + flags[1]
    small[1].wait()
    for g in range(heads):
        queries[me, g * steps:(g + 1) * steps, :] = query_ref[:, g * HEAD:(g + 1) * HEAD]

    barrier = pltpu.get_barrier_semaphore()
    near = z * group
    xc = x * 2 + c
    for r in range(1, group):
        pl.semaphore_signal(barrier, inc=1, device_id=(near + (xc + r) % group, tp), device_id_type=MESH)
    for d in range(1, nz):
        pl.semaphore_signal(barrier, inc=1, device_id=(dev((z + d) % nz, x, c), tp), device_id_type=MESH)
    for d in range(1, ny):
        pl.semaphore_signal(barrier, inc=1, device_id=(me, (tp + d) % ny), device_id_type=MESH)
    pl.semaphore_wait(barrier, group - 1 + nz - 1 + ny - 1)

    def counts_near(r):
        return remote(counts.at[me], counts.at[me], 0, c1_recv, near + (xc + r) % group)

    def counts_far(d):
        part = pl.ds(near, group)
        return remote(counts.at[part], counts.at[part], 1, c2_recv, dev((z + d) % nz, x, c))

    def totals_out(d):
        return remote(totals.at[tp], totals.at[tp], 2, t_recv, me, (tp + d) % ny)

    def query(slot, recv, where):
        return remote(queries.at[slot], queries.at[slot], 3, recv, where)

    def query_z(i):
        return query(me, qz_recv.at[i], dev((z - far(i) + nz) % nz, x, c))

    def query_z_in(i):
        slot = dev((z + far(i)) % nz, x, c)
        return query(slot, qz_recv.at[i], slot)

    def query_x(i, d):
        return query(dev((z + far(i)) % nz, x, c), qx_recv.at[i], dev(z, (x + d) % nx, c))

    def query_c(i, d):
        slot = dev((z + far(i)) % nz, (x - d + nx) % nx, c)
        return query(slot, qc_recv.at[i], dev(z, x, sib))

    def forward_z(i):
        for d in range(1, nx):
            query_x(i, d).start()
        query_c(i, 0).start()

    def forward_x(i):
        drain(queries.at[pl.ds(0, nx - 1)], qx_recv.at[i])
        for d in range(1, nx):
            query_c(i, d).start()

    for r in range(1, group):
        counts_near(r).start()
    for i in range(nz - 1):
        query_z(i).start()
    forward_z(nz - 1)
    drain(counts.at[pl.ds(0, group - 1)], c1_recv)
    for d in range(1, nz):
        counts_far(d).start()
    for i in range(nz - 1):
        query_z_in(i).wait_recv()
        forward_z(i)
    drain(counts.at[pl.ds(0, (nz - 1) * group)], c2_recv)

    before = jnp.zeros((1, seqs), F32)
    total = jnp.zeros((1, seqs), F32)
    for j in range(seqs):
        row = counts[j]
        total = total + row
        before = before + jnp.where(j < me, row, 0.0)
    totals[tp] = total
    for d in range(1, ny):
        totals_out(d).start()

    freq = freq_ref[...]
    lane = lax.broadcasted_iota(jnp.int32, (1, HEAD), 1)
    sign = jnp.where(lane < HEAD // 2, -1.0, 1.0).astype(F32)

    def down(row):
        return jnp.transpose(jnp.broadcast_to(row, (HEAD, seqs)))

    slot0 = before
    slot1 = before + flags[0]
    first_block = (2 * me).astype(F32)
    for j, slot in enumerate((slot0, slot1)):
        angle = (down(slot) - (first_block + j)) * float(BLOCK) * freq
        table[2 * j] = jnp.cos(angle)
        table[2 * j + 1] = jnp.sin(angle) * sign
        live[j] = down(flags[j])

    def rotate_keys(k, carry):
        for i, j in ((2 * k, 0), (2 * k, 1), (2 * k + 1, 0), (2 * k + 1, 1)):
            cosine = table[2 * j, pl.ds(i, 1), :]
            sine = table[2 * j + 1, pl.ds(i, 1), :]
            part = pl.ds(j * BLOCK, BLOCK)
            packed = keys[i, part, :]
            swapped = pltpu.roll(packed, HEAD // 2, 1).astype(F32)
            turned = packed.astype(F32) * cosine + swapped * sine
            keys[i, part, :] = turned.astype(BF16)
        return carry

    for i in range(chunks):
        load(i).wait()
        lax.fori_loop(i * chunk // 2, (i + 1) * chunk // 2, rotate_keys, 0)
    load_values.wait()

    for copy in small[2:]:
        copy.wait()

    longest = total
    drain(totals.at[pl.ds(0, ny - 1)], t_recv)
    for d in range(1, ny):
        longest = jnp.maximum(longest, totals[(tp + d) % ny])
    angle = down(longest) * float(BLOCK) * freq
    table[4] = jnp.cos(angle)
    table[5] = jnp.sin(angle)
    step_angle = lax.broadcasted_iota(jnp.int32, (steps, HEAD), 0).astype(F32) * freq
    step_cos = jnp.cos(step_angle)
    step_sin = jnp.sin(step_angle)

    def step_turn(s):
        cosine = table[4, pl.ds(s, 1), :]
        sine = table[5, pl.ds(s, 1), :]
        return (
            cosine * step_cos - sine * step_sin,
            (sine * step_cos + cosine * step_sin) * sign,
        )

    def turn_queries(slot, s):
        cosine, sine = step_turn(s)
        stored = queries[slot].astype(F32)
        swapped = pltpu.roll(stored, HEAD // 2, 1)
        shape = (heads, steps, HEAD)
        turned = stored.reshape(shape) * cosine[None] + swapped.reshape(shape) * sine[None]
        return turned.reshape(rows, HEAD).astype(BF16)

    def contract(a, b, dims):
        return lax.dot_general(a, b, (dims, ((), ())), preferred_element_type=F32)

    def shifted(m):
        return m.astype(BF16).astype(F32)

    def partials(slots):
        places = [owner_ref[slot] for slot in slots]
        turned = [turn_queries(slot, s) for slot, s in zip(slots, places)]
        scores = [contract(keys[s], q, ((1,), (1,))) * score_scale for s, q in zip(places, turned)]
        kept = [[live[j, pl.ds(s, 1), :] > 0.5 for j in range(2)] for s in places]
        pieces = [[a[j * BLOCK:(j + 1) * BLOCK] for j in range(2)] for a in scores]
        tops = [
            [jnp.where(k[j], jnp.max(a[j], axis=0, keepdims=True), NEG) for j in range(2)]
            for k, a in zip(kept, pieces)
        ]
        m = [shifted(jnp.maximum(*t)) for t in tops]
        weights = [
            [jnp.exp2(a[j] - jnp.where(k[j], b, -NEG)) for j in range(2)]
            for k, a, b in zip(kept, pieces, m)
        ]
        l = [jnp.sum(w[0] + w[1], axis=0, keepdims=True) for w in weights]
        o = [
            contract(values[s], jnp.concatenate(w, axis=0).astype(BF16), ((0,), (0,)))
            for s, w in zip(places, weights)
        ]
        return list(zip(m, l, o))

    sub8 = lax.broadcasted_iota(jnp.int32, (8, HEAD), 0)
    sub16 = lax.broadcasted_iota(jnp.int32, (16, HEAD), 0)

    def put(ref, m, l, o):
        ref[0:HEAD, :] = o
        ref[HEAD:HEAD + 8, :] = jnp.where(sub8 == 0, m, l)

    def get(ref):
        tail = ref[HEAD:HEAD + 8, :]
        return tail[0:1], tail[1:2], ref[0:HEAD, :]

    def put_half(ref, m, l, o):
        high = l.astype(BF16).astype(F32)
        ref[0:HEAD, :] = o.astype(BF16)
        tail = jnp.where(sub16 == 0, m, jnp.where(sub16 == 1, high, l - high))
        ref[HEAD:HEAD + 16, :] = tail.astype(BF16)

    def get_half(ref):
        tail = ref[HEAD:HEAD + 16, :].astype(F32)
        return tail[0:1], tail[1:2] + tail[2:3], ref[0:HEAD, :].astype(F32)

    def merge(parts):
        m = functools.reduce(jnp.maximum, [p[0] for p in parts])
        scales = [jnp.exp2(p[0] - m) for p in parts]
        l = functools.reduce(jnp.add, [p[1] * a for p, a in zip(parts, scales)])
        o = functools.reduce(jnp.add, [p[2] * a for p, a in zip(parts, scales)])
        return m, l, o

    def pair_copy(i):
        return remote(pair_out.at[i], pair_in.at[i], 4, pair_recv.at[i], dev(z, x, sib))

    def x_copy(i, d):
        return remote(x_out.at[i, d - 1], x_in.at[i, d - 1], 5, x_recv.at[i],
                      dev(z, (x + d) % nx, c))

    def z_copy(i):
        return remote(z_out.at[i], z_in.at[i], 6, z_recv.at[i], dev((z + far(i)) % nz, x, c))

    def stage_partials(i):
        z_ = (z + far(i)) % nz
        drain(queries.at[pl.ds(0, nx)], qc_recv.at[i])
        for d, part in enumerate(partials([dev(z_, (x + d) % nx, sib) for d in range(nx)])):
            put(pair_out.at[i, d], *part)
        pair_copy(i).start()

        @pl.when(i >= 1)
        def _():
            stage_x(i - 1)

        for d, part in enumerate(partials([dev(z_, (x + d) % nx, c) for d in range(nx)])):
            put(pair_own.at[i, d], *part)

    def stage_x(i):
        pair_copy(i).wait_recv()
        for d in range(nx):
            merged = merge([get(pair_own.at[i, d]), get(pair_in.at[i, d])])
            if d == 0:
                put(x_own.at[i], *merged)
            else:
                put_half(x_out.at[i, d - 1], *merged)
                x_copy(i, d).start()

    def stage_z(i):
        drain(x_in.at[i], x_recv.at[i])
        return merge([get(x_own.at[i])] + [get_half(x_in.at[i, d]) for d in range(nx - 1)])

    def send_z(i):
        put_half(z_out.at[i], *stage_z(i))
        z_copy(i).start()

    forward_x(0)
    forward_x(1)

    def step(i, carry):
        @pl.when(i < nz - 2)
        def _():
            forward_x(i + 2)

        @pl.when(i < nz)
        def _():
            stage_partials(i)

        @pl.when(i == nz)
        def _():
            stage_x(i - 1)

        @pl.when((i >= lag) & (i - lag < nz - 1))
        def _():
            send_z(i - lag)

        return carry

    lag = min(LAG, nz)
    lax.fori_loop(0, nz + 1, step, 0)

    s = owner_ref[me]
    turned = turn_queries(me, s)
    cosine, sine = step_turn(s)
    fresh = newk_ref[...].astype(F32)
    fresh = (fresh * cosine + pltpu.roll(fresh, HEAD // 2, 1) * sine).astype(BF16)
    scores = contract(fresh, turned, ((1,), (1,))) * score_scale
    row_step = lax.broadcasted_iota(jnp.int32, (steps, rows), 1) % steps
    causal = lax.broadcasted_iota(jnp.int32, (steps, rows), 0) <= row_step
    scores = jnp.where(causal, scores, NEG)
    m = shifted(jnp.max(scores, axis=0, keepdims=True))
    weights = jnp.where(causal, jnp.exp2(scores - m), 0.0)
    l = jnp.sum(weights, axis=0, keepdims=True)
    fresh = (m, l, contract(newv_ref[...], weights.astype(BF16), ((0,), (0,))))

    for i in range(nz + 1 - lag, nz - 1):
        send_z(i)
    parts = [fresh]
    parts.append(stage_z(nz - 1))
    for i in range(nz-1):
        z_copy(i).wait_recv()
        parts.append(get_half(z_in.at[i]))
    m, l, o = merge(parts)
    result = jnp.transpose(o / l).astype(BF16)
    for g in range(heads):
        out_ref[:, g * HEAD:(g + 1) * HEAD] = result[g * steps:(g + 1) * steps]

    for kind, ref in enumerate((
        counts.at[pl.ds(0, group - 1)], counts.at[pl.ds(0, (nz - 1) * group)], totals.at[pl.ds(0, ny - 1)],
        queries.at[pl.ds(0, seqs - 1)], pair_out, x_out, z_out,
    )):
        drain(ref, send_sem.at[kind])


def shards(
    nz, nx, ny,
    prompt_keys, prompt_values, keep_mask, owner_sequence, step_queries, new_keys, new_values,
):
    seqs = prompt_keys.shape[0]
    steps = step_queries.shape[1]
    freq = frequencies(HEAD // 2)
    freq = jnp.concatenate([freq, freq])[None]
    hbm = pl.BlockSpec(memory_space=pltpu.HBM)
    vmem = pl.BlockSpec(memory_space=pltpu.VMEM)
    dma = pltpu.SemaphoreType.DMA
    group = nx * 2
    out = pl.pallas_call(
        functools.partial(kernel, nz, nx, ny),
        out_shape=jax.ShapeDtypeStruct((steps, step_queries.shape[3]), BF16),
        in_specs=[hbm, hbm, vmem] + [hbm] * 5,
        out_specs=vmem,
        scratch_shapes=[
            pltpu.SMEM((seqs,), jnp.int32),
            pltpu.VMEM((2, 1, seqs), jnp.int32),
            pltpu.VMEM((steps, step_queries.shape[3]), BF16),
            pltpu.VMEM((steps, HEAD), BF16),
            pltpu.VMEM((steps, HEAD), BF16),
            pltpu.VMEM((seqs, 2 * BLOCK, HEAD), BF16),
            pltpu.VMEM((seqs, 2 * BLOCK, HEAD), BF16),
            pltpu.VMEM((seqs, HEAD, HEAD), BF16),
            pltpu.VMEM((seqs + 8, 1, seqs), F32),
            pltpu.VMEM((ny + 8, 1, seqs), F32),
            pltpu.VMEM((7, seqs, HEAD), F32),
            pltpu.VMEM((3, seqs, HEAD), F32),
            pltpu.VMEM((nz, nx, HEAD + 8, HEAD), F32),
            pltpu.VMEM((nz, nx, HEAD + 8, HEAD), F32),
            pltpu.VMEM((nz, nx, HEAD + 8, HEAD), F32),
            pltpu.VMEM((nz, nx - 1, HEAD + 16, HEAD), BF16),
            pltpu.VMEM((nz, nx - 1, HEAD + 16, HEAD), BF16),
            pltpu.VMEM((nz, HEAD + 8, HEAD), F32),
            pltpu.VMEM((nz - 1, HEAD + 16, HEAD), BF16),
            pltpu.VMEM((nz - 1, HEAD + 16, HEAD), BF16),
            dma((5,)), dma((5,)), dma((7,)), dma, dma, dma,
            dma((nz,)), dma((nz,)), dma((nz,)), dma((nz,)), dma((nz,)), dma((nz,)),
        ],
        compiler_params=pltpu.CompilerParams(
            collective_id=0, has_side_effects=True, vmem_limit_bytes=64 * 1024 * 1024
        ),
    )(
        owner_sequence, keep_mask.transpose(1, 2, 0), freq, step_queries[0, :, 0], new_keys[0],
        new_values[0],
        prompt_keys, prompt_values,
    )
    return out[None, :, None]


def solution(mesh):
    in_specs = (
        P(None, "seq", "tp"),
        P(None, "seq", "tp"),
        P(None, "seq", "tp"),
        P(),
        P("seq", None, "tp", None),
        P("seq", None, "tp"),
        P("seq", None, "tp"),
    )
    out_specs = P("seq", None, "tp", None)
    seq = mesh.shape["seq"]
    nx = 4 if seq >= 64 else 2
    body = functools.partial(shards, seq // (2 * nx), nx, mesh.shape["tp"])
    return jax.shard_map(body, mesh=mesh, in_specs=in_specs, out_specs=out_specs, check_vma=False)
```
